128 devices in a mesh: group: 8 (over x_lo, z), blk: 16 (over y, x_hi, core).
Axes of the slice: x: 4 (x_hi: 2, x_lo: 2; x = x_hi * 2 + x_lo), y: 4, z: 4, core: 2. Of those that a mesh axis runs over, the one named last changes fastest.
Arguments:
- cotangent: bfloat16 [98304, 3584], P(('group', 'blk')), may hold values from -24 to 24
- pre_act: bfloat16 [98304, 2, 1024], P(('group', 'blk')), may hold values from -6 to 6
- down_weight: bfloat16 [1024, 2, 3584], P('blk'), may hold values from -0.09375 to 0.09375
- tile_expert: int32 [768], P(('group', 'blk')), may hold values from 0 to 1
- tile_fill: int32 [768], P(('group', 'blk')), may hold values from 1 to 128, as said below
Outputs:
- act_grad: bfloat16 [98304, 2, 1024], P(('group', 'blk'))
- weight_grad: float32 [1024, 2, 3584], P(('group', 'blk'))
The draws below stay inside these ranges and needn't reach their ends.
Inputs may be any that keep to these rules, and one draw needn't show every extreme that they name: tile_fill reaches 128 in every draw.
All inputs are finite; a program needn't handle non-finite values.
Results may differ from the reference program's by a relative error of at most 0.0029.
Values may be sent and summed in bfloat16 or wider, within the bound.
A program may use at most 192 MiB of HBM per device.

```python
import jax
import jax.numpy as jnp
from jax import lax

D = 3584
H = 1024
EXPERTS = 2
TILE = 128
TILES = 6
TILES_ALL = 768
ROWS_ALL = 98304
N_GROUP = 8
N_BLK = 16


def draw_tile_fill(key, part):
    fill_values = jax.random.randint(key, (TILES_ALL,), 1, TILE + 1)
    return fill_values.at[0].set(TILE).astype(jnp.int32)


def plant(entries, rng, smallest, top_value):
    dims = entries.shape
    spot = [jax.random.randint(jax.random.fold_in(rng, axis), (), 0, dims[axis]) for axis in range(len(dims))]
    entries = entries.at[tuple(spot)].set(smallest)
    longest = dims.index(max(dims))
    spot[longest] = (spot[longest] + 1) % dims[longest]
    return entries.at[tuple(spot)].set(top_value)


def with_spikes(array, rng, source, target, shards_of, factor):
    owner, partner = [(jnp.arange(array.shape[dim]) // (array.shape[dim] // shards_of)).reshape([-1 if axis == dim else 1 for axis in range(array.ndim)]) for dim in (source, target)]
    chosen = jax.random.permutation(rng, shards_of)[partner]
    strong = (owner == chosen) | (owner == (partner + shards_of // 2) % shards_of)
    return jnp.where(strong, factor * array, array)


def steps_of(own_key, extent, cuts, smallest, largest):
    factor_of = 1.0
    for position, blocks in cuts:
        steps = jax.random.uniform(jax.random.fold_in(jax.random.fold_in(own_key, 6), position), (blocks,), jnp.float32, smallest / len(cuts), largest / len(cuts))
        factor_of = factor_of * jnp.repeat(jnp.exp(steps), extent[position] // blocks).reshape((-1,) + (1,) * (len(extent) - 1 - position))
    return factor_of


def normal_values(key, dims, scale, reach, pieces=(), held_as=jnp.bfloat16):
    factor_of = steps_of(key, dims, pieces, -0.22, 0.18) if pieces else 1.0
    result = jax.random.normal(key, dims, jnp.float32) * scale * factor_of
    return jnp.minimum(jnp.maximum(result, -reach), reach).astype(held_as)


def gaussian_with(stream_key, dims, spread, reach, cuts, heavy, kind=jnp.bfloat16):
    values = spread * jax.random.normal(stream_key, dims, jnp.float32)
    if cuts:
        values = values * steps_of(stream_key, dims, cuts, -0.22, 0.18)
    return jnp.clip(with_spikes(values, jax.random.fold_in(stream_key, 3), *heavy), -reach, reach).astype(kind)


def setup_inputs(seed: int = 0) -> dict:
    streams_of = jax.random.split(jax.random.key(seed), 6)
    cotangent = gaussian_with(streams_of[0], (ROWS_ALL, D), 1.0, 24.0, ((0, 128),), (0, 1, 128, 5.5))
    pre_act = normal_values(streams_of[1], (ROWS_ALL, 2, H), 1.5, 6.0, ((0, 128),))
    down_weight = normal_values(streams_of[2], (H, EXPERTS, D), D ** -0.5, 0.09375, ((0, 16),))
    tile_expert = plant(jax.random.randint(streams_of[3], (TILES_ALL,), 0, EXPERTS), jax.random.fold_in(streams_of[3], 1), 0, EXPERTS - 1).astype(jnp.int32)
    tile_fill = draw_tile_fill(jax.random.fold_in(streams_of[5], 71), 0)
    return {"cotangent": cotangent, "pre_act": pre_act, "down_weight": down_weight, "tile_expert": tile_expert, "tile_fill": tile_fill}


grad_factor = 0.015625


def reference(cotangent, pre_act, down_weight, tile_expert, tile_fill):
    device_count = N_GROUP * N_BLK
    cot_all = cotangent.reshape(device_count, TILES, TILE, D)
    pre_all = pre_act.reshape(device_count, TILES, TILE, 2, H)
    expert_all = tile_expert.reshape(device_count, TILES)
    fill_all = tile_fill.reshape(device_count, TILES)

    def one_device(total, item):
        cot_tiles, pre_tiles, expert_ids, fill_values = item
        chosen = jnp.take(down_weight, expert_ids, axis=1).astype(jnp.float32)
        hidden_grad = jnp.einsum("trd,htd->trh", cot_tiles.astype(jnp.float32), chosen)
        live_rows = (jnp.arange(TILE, dtype=jnp.int32)[None, :] < fill_values[:, None]).astype(jnp.float32)[:, :, None]
        gate_pre = pre_tiles[:, :, 0, :].astype(jnp.float32)
        up_pre = pre_tiles[:, :, 1, :].astype(jnp.float32)
        sigmoid_gate = jax.nn.sigmoid(gate_pre)
        silu_gate = gate_pre * sigmoid_gate
        activation = (live_rows * silu_gate * up_pre).astype(jnp.bfloat16)
        gate_grad = live_rows * hidden_grad * up_pre * sigmoid_gate * (1.0 + gate_pre * (1.0 - sigmoid_gate))
        up_grad = live_rows * hidden_grad * silu_gate
        grads = jnp.stack([gate_grad, up_grad], axis=2).astype(jnp.bfloat16)
        per_tile = jnp.einsum("trh,trd->thd", activation.astype(jnp.float32), cot_tiles.astype(jnp.float32))
        expert_hot = (expert_ids[:, None] == jnp.arange(EXPERTS, dtype=jnp.int32)[None, :]).astype(jnp.float32)
        term = jnp.einsum("te,thd->hed", expert_hot, per_tile)
        return total + term, grads

    start_total = jnp.zeros((H, EXPERTS, D), jnp.float32)
    total, grads = lax.scan(one_device, start_total, (cot_all, pre_all, expert_all, fill_all))
    return grads.reshape(ROWS_ALL, 2, H), total * grad_factor
```

```python
import functools

import jax
import jax.numpy as jnp
from jax import lax
from jax.experimental import pallas as pl
from jax.experimental.pallas import tpu as pltpu
from jax.sharding import PartitionSpec as P

MESH = pl.DeviceIdType.MESH
grad_factor = 0.015625

ROWS = 768
WIDTH = 3584
WIDE = 512
CHUNKS = WIDTH // WIDE
COLS = 256
STAGE_ROWS = (256, 64, 16)
STAGE_TYPES = (jnp.bfloat16, jnp.bfloat16, jnp.float32)
f32 = jnp.float32


def kernel(
    cot_hbm, lhs_hbm, w_hbm, hot_ref,
    hidden_hbm, wgrad_hbm,
    cot_own, cot_sib, lhs, w_all, hg_buf, out_buf,
    own0, own1, own2, rel0, rel1, rel2, tot0, tot1,
    far0, far1, far2, up0, up1, up2, dn0, dn1, dn2,
    rfar0, rfar1, rfar2, rup0, rup1, rup2, rdn0, rdn1, rdn2,
    cot_sem, lhs_sem, w_sem, hg_sem, out_sem,
    cs_send, cs_recv, ls_send, ls_recv,
    ag_send, ag_recv, sib_send, sib_recv,
    s0_send, s0_recv, s1_send, s1_recv, s2_send, s2_recv,
):
    g = lax.axis_index("group")
    b = lax.axis_index("blk")
    x_lo, z = lax.div(g, 4), lax.rem(g, 4)
    y, c = lax.div(b, 4), lax.rem(b, 2)
    x_hi = lax.rem(lax.div(b, 2), 2)
    x = x_hi * 2 + x_lo

    def device(dx, dy, dz, core):
        xx, yy, zz = lax.rem(x + dx, 4), lax.rem(y + dy, 4), lax.rem(z + dz, 4)
        return (lax.rem(xx, 2) * 4 + zz, yy * 4 + lax.div(xx, 2) * 2 + core)

    other = 1 - c
    sibling = device(0, 0, 0, other)
    x_up, x_dn = device(1, 0, 0, c), device(3, 0, 0, c)
    y_up, y_dn = device(0, 1, 0, c), device(0, 3, 0, c)
    z_up, z_dn = device(0, 0, 1, c), device(0, 0, 3, c)
    x_peer = device(3 - 2 * x + 4, 0, 0, c)

    barrier = pltpu.get_barrier_semaphore()
    for peer in (sibling, x_up, x_dn, y_up, y_dn, z_up, z_dn):
        pl.semaphore_signal(barrier, inc=1, device_id=peer, device_id_type=MESH)

    def cot_cols(k):
        return pl.ds(pl.multiple_of(k * WIDE, WIDE), WIDE)

    def cot_copy(k):
        return pltpu.make_async_copy(cot_hbm.at[:, cot_cols(k)], cot_own.at[:, cot_cols(k)], cot_sem.at[k])

    def lhs_copy():
        return pltpu.make_async_copy(lhs_hbm.at[c], lhs.at[0], lhs_sem)

    q_own = y * 2 + x_hi

    def w_copy(e):
        return pltpu.make_async_copy(w_hbm.at[e], w_all.at[q_own, e, c], w_sem.at[e])

    for e in range(2):
        w_copy(e).start()
    lhs_copy().start()

    @pl.loop(0, CHUNKS)
    def _(k):
        cot_copy(k).start()

    pl.semaphore_wait(barrier, 7)

    def remote(src, dst, send, recv, device_id):
        return pltpu.make_async_remote_copy(
            src_ref=src, dst_ref=dst, send_sem=send, recv_sem=recv, device_id=device_id, device_id_type=MESH
        )

    def lhs_remote():
        return remote(lhs_hbm.at[other], lhs.at[1], ls_send, ls_recv, sibling)

    def cot_remote(k):
        return remote(
            cot_hbm.at[:, cot_cols(k)], cot_sib.at[:, cot_cols(k)], cs_send.at[k], cs_recv.at[k], sibling
        )

    def piece(j):
        yy = lax.rem(y + (0, 3, 1, 2)[j % 4], 4)
        return yy * 2 + (x_hi if j < 4 else 1 - x_hi)

    def gather(src_j, dst_j, e, slot, device_id):
        block = w_all.at[piece(src_j), e, c]
        return remote(block, block, ag_send.at[slot], ag_recv.at[dst_j, e], device_id)

    def gather_wait(j, e):
        block = w_all.at[piece(j), e, c]
        remote(block, block, ag_send.at[0], ag_recv.at[j, e], sibling).wait_recv()

    def share(j, e):
        block = w_all.at[piece(j), e, c]
        return remote(block, block, sib_send.at[j, e], sib_recv.at[j, e], sibling)

    def share_wait(j, e):
        block = w_all.at[piece(j), e, other]
        remote(block, block, sib_send.at[j, e], sib_recv.at[j, e], sibling).wait_recv()

    sends = []
    for e in range(2):
        sends += [(0, 1, e, y_up), (0, 2, e, y_dn), (0, 4, e, x_peer)]
    sends += [(1, 3, 0, y_up), (2, 3, 1, y_dn)]
    for e in range(2):
        sends += [(4, 5, e, y_up), (4, 6, e, y_dn)]
    sends += [(5, 7, 0, y_up), (6, 7, 1, y_dn)]

    def gather_start(j):
        for slot, (src, dst, e, device_id) in enumerate(sends):
            if src == j:
                gather(src, dst, e, slot, device_id).start()

    def arrived(j):
        for e in range(2):
            gather_wait(j, e)
        gather_start(j)
        for e in range(2):
            share(j, e).start()

    lhs_remote().start()
    cot_remote(0).start()
    for e in range(2):
        w_copy(e).wait()
    gather_start(0)

    @pl.loop(1, CHUNKS)
    def _(k):
        cot_remote(k).start()

    for e in range(2):
        share(0, e).start()

    own, rel, tot = (own0, own1, own2), (rel0, rel1, rel2), (tot0, tot1)
    far, up, dn = (far0, far1, far2), (up0, up1, up2), (dn0, dn1, dn2)
    rfar, rup, rdn = (rfar0, rfar1, rfar2), (rup0, rup1, rup2), (rdn0, rdn1, rdn2)
    s_send, s_recv = (s0_send, s1_send, s2_send), (s0_recv, s1_recv, s2_recv)
    z_ring, x_ring, y_ring = (z, z_up, z_dn), (x, x_up, x_dn), (y, y_up, y_dn)
    rings = ((z_ring, x_ring, y_ring), (x_ring, z_ring, y_ring))

    def far_copy(s, st, n, half):
        rows = STAGE_ROWS[s] // 2
        _, plus, minus = rings[st][s]
        return remote(
            far[s].at[n, pl.ds(half * rows, rows)], rfar[s].at[n, pl.ds(half * rows, rows)],
            s_send[s].at[n, half], s_recv[s].at[n, half], (plus, minus)[half],
        )

    def near_copy(s, st, n, way):
        _, plus, minus = rings[st][s]
        return remote(
            (up, dn)[way][s].at[n], (rup, rdn)[way][s].at[n],
            s_send[s].at[n, 2 + way], s_recv[s].at[n, 2 + way], (plus, minus)[way],
        )

    def produce(s, st, n, block):
        half = STAGE_ROWS[s] // 2
        kind = STAGE_TYPES[s]
        far[s][n] = block(2).astype(kind)
        far_copy(s, st, n, 0).start()
        far_copy(s, st, n, 1).start()
        value = block(1)
        rel[s][lax.rem(n, 4), 0] = value[:half]
        up[s][n, half:] = value[half:].astype(kind)
        value = block(3)
        rel[s][lax.rem(n, 4), 1] = value[half:]
        dn[s][n, :half] = value[:half].astype(kind)
        own[s][n] = block(0)

    def relay(s, st, n):
        half = STAGE_ROWS[s] // 2
        kind = STAGE_TYPES[s]
        far_copy(s, st, n, 0).wait_recv()
        up[s][n, :half] = (rel[s][lax.rem(n, 4), 0] + rfar[s][n, :half].astype(f32)).astype(kind)
        near_copy(s, st, n, 0).start()
        far_copy(s, st, n, 1).wait_recv()
        dn[s][n, half:] = (rel[s][lax.rem(n, 4), 1] + rfar[s][n, half:].astype(f32)).astype(kind)
        near_copy(s, st, n, 1).start()

    def total(s, st, n):
        near_copy(s, st, n, 0).wait_recv()
        near_copy(s, st, n, 1).wait_recv()
        return own[s][n] + rup[s][n].astype(f32) + rdn[s][n].astype(f32)

    def first(st, k):
        cols = pl.ds(pl.multiple_of(k * WIDE + st * COLS, COLS), COLS)
        me = (z, x)[st]

        def block(offset):
            at = lax.rem(me + offset, 4)
            value = None
            for src, cot in ((0, cot_own), (1, cot_sib)):
                rows = lhs[src, at] if st == 0 else lhs[src, :, at]
                part = jnp.dot(rows.reshape(256, ROWS), cot[:, cols], preferred_element_type=f32)
                value = part if value is None else value + part
            return value

        produce(0, st, k * 2 + st, block)

    def onward(s, st, n):
        tot[s][st] = total(s, st, n)
        me = rings[st][s + 1][0]
        rows = STAGE_ROWS[s + 1]

        def block(offset):
            at = lax.rem(me + offset, 4) * rows
            return tot[s][st, pl.ds(pl.multiple_of(at, rows), rows), :]

        produce(s + 1, st, n, block)

    def last(st, n):
        cols = pl.ds(pl.multiple_of(n * COLS, COLS), COLS)
        out_buf[:, cols] = total(2, st, n) * grad_factor

    order = (0, 1, 2, 4, 3, 5, 6, 7)

    def hg_copy(turn):
        cols = pl.ds(pl.multiple_of(piece(order[turn]) * 128, 128), 128)
        return pltpu.make_async_copy(hg_buf.at[turn % 2], hidden_hbm.at[:, cols], hg_sem.at[turn])

    def hidden(turn):
        j = order[turn]
        for e in range(2):
            share_wait(j, e)
        if turn >= 2:
            hg_copy(turn - 2).wait()
        q = piece(j)

        @pl.loop(0, ROWS // 256)
        def _(m):
            rows = pl.ds(pl.multiple_of(m * 256, 256), 256)
            each = lax.dot_general(
                cot_own[rows, :], w_all[q].reshape(256, WIDTH), (((1,), (1,)), ((), ())), preferred_element_type=f32
            )
            hg_buf[turn % 2, rows, :] = jnp.where(hot_ref[rows, :] > 0.5, each[:, 128:], each[:, :128])

        hg_copy(turn).start()

    lhs_copy().wait()
    lhs_remote().wait_recv()

    events = {3: "12", 4: "4", 6: "3", 7: "56", 9: "7"}
    turns = {6: (0,), 7: (1,), 8: (2,), 9: (3, 4), 10: (5,), 11: (6,), 12: (7,)}

    @pl.loop(0, CHUNKS + 6)
    def _(t):
        def at(lag, do):
            @pl.when(jnp.logical_and(t >= lag, t < CHUNKS + lag))
            def _():
                do(t - lag)

        def make(k):
            cot_copy(k).wait()
            cot_remote(k).wait_recv()
            for st in range(2):
                first(st, k)

        def both(do):
            def run(k):
                for st in range(2):
                    do(st, k * 2 + st)

            return run

        at(0, make)
        at(1, both(lambda st, n: relay(0, st, n)))
        at(2, both(lambda st, n: onward(0, st, n)))
        at(3, both(lambda st, n: relay(1, st, n)))
        at(4, both(lambda st, n: onward(1, st, n)))
        at(5, both(lambda st, n: relay(2, st, n)))
        at(6, both(last))
        def on(when, do):
            @pl.when(t == when)
            def _():
                do()

        for when in range(CHUNKS + 6):
            for j in events.get(when, ""):
                on(when, functools.partial(arrived, int(j)))
            for turn in turns.get(when, ()):
                on(when, functools.partial(hidden, turn))

    out = pltpu.make_async_copy(out_buf, wgrad_hbm, out_sem)
    out.start()
    for turn in (6, 7):
        hg_copy(turn).wait()
    out.wait()

    lhs_remote().wait_send()

    @pl.loop(0, CHUNKS)
    def _(k):
        cot_remote(k).wait_send()
        for st in range(2):
            for s in range(3):
                for i in range(2):
                    far_copy(s, st, k * 2 + st, i).wait_send()
                    near_copy(s, st, k * 2 + st, i).wait_send()

    for slot, (src, dst, e, device_id) in enumerate(sends):
        gather(src, dst, e, slot, device_id).wait_send()
    for j in range(8):
        for e in range(2):
            share(j, e).wait_send()


def call(cot, lhs, w, hot):
    n = 2 * CHUNKS
    dma = pltpu.SemaphoreType.DMA
    any_space = pl.BlockSpec(memory_space=pl.ANY)

    def stages(shape, kind=None):
        return [pltpu.VMEM(shape(r), kind or t) for r, t in zip(STAGE_ROWS, STAGE_TYPES)]

    return pl.pallas_call(
        kernel,
        out_shape=(
            jax.ShapeDtypeStruct((ROWS, 1024), f32),
            jax.ShapeDtypeStruct((16, WIDTH), f32),
        ),
        in_specs=[any_space, any_space, any_space, pl.BlockSpec(memory_space=pltpu.VMEM)],
        out_specs=(any_space, any_space),
        scratch_shapes=[
            pltpu.VMEM((ROWS, WIDTH), jnp.bfloat16),
            pltpu.VMEM((ROWS, WIDTH), jnp.bfloat16),
            pltpu.VMEM((2, 4, 4, 64, ROWS), jnp.bfloat16),
            pltpu.VMEM((8, 2, 2, 64, WIDTH), jnp.bfloat16),
            pltpu.VMEM((2, ROWS, 128), f32),
            pltpu.VMEM((16, WIDTH), f32),
            *stages(lambda r: (n, r, COLS), f32),
            *stages(lambda r: (4, 2, r // 2, COLS), f32),
            *[pltpu.VMEM((2, r, COLS), f32) for r in STAGE_ROWS[:2]],
            *stages(lambda r: (n, r, COLS)),
            *stages(lambda r: (n, r, COLS)),
            *stages(lambda r: (n, r, COLS)),
            *stages(lambda r: (n, r, COLS)),
            *stages(lambda r: (n, r, COLS)),
            *stages(lambda r: (n, r, COLS)),
            dma((CHUNKS,)), dma, dma((2,)), dma((8,)), dma,
            dma((CHUNKS,)), dma((CHUNKS,)), dma, dma,
            dma((14,)), dma((8, 2)), dma((8, 2)), dma((8, 2)),
            dma((n, 4)), dma((n, 4)), dma((n, 4)), dma((n, 4)), dma((n, 4)), dma((n, 4)),
        ],
        compiler_params=pltpu.CompilerParams(
            collective_id=0, has_side_effects=True, vmem_limit_bytes=60 * 2**20
        ),
        cost_estimate=pl.CostEstimate(flops=24 * 10**9, bytes_accessed=30 * 10**6, transcendentals=0),
    )(cot, lhs, w, hot)


def body(cotangent, pre_act, down_weight, tile_expert, tile_fill):
    row_count = cotangent.shape[0]
    tile_count = tile_expert.shape[0]
    tile_size = row_count // tile_count
    expert_count = down_weight.shape[1]
    positions = jnp.arange(tile_size, dtype=jnp.int32)
    live_rows = (positions[None, :] < tile_fill[:, None]).astype(f32).reshape(row_count, 1)
    row_expert = jnp.repeat(tile_expert, tile_size)
    gate_pre = pre_act[:, 0, :].astype(f32)
    up_pre = pre_act[:, 1, :].astype(f32)
    sigmoid_gate = jax.nn.sigmoid(gate_pre)
    silu_gate = gate_pre * sigmoid_gate
    activation = (live_rows * silu_gate * up_pre).astype(jnp.bfloat16)
    parts = activation.reshape(row_count, 2, 4, 4, 2, 2, 8).transpose(5, 2, 4, 1, 3, 6, 0)
    expert_hot = row_expert[None, :] == jnp.arange(expert_count, dtype=jnp.int32)[:, None]
    lhs = jnp.where(expert_hot[:, None, :], parts[:, :, :, :, :, None], jnp.zeros((), jnp.bfloat16))
    lhs = lhs.reshape(2, 4, 4, 64, row_count)
    weights = jnp.swapaxes(down_weight, 0, 1)
    hot = jnp.broadcast_to((row_expert == 1).astype(f32)[:, None], (row_count, 128))
    hidden_grad, partial = call(cotangent, lhs, weights, hot)
    gate_grad = (
        live_rows * hidden_grad * up_pre * sigmoid_gate * (1.0 + gate_pre * (1.0 - sigmoid_gate))
    )
    up_grad = live_rows * hidden_grad * silu_gate
    act_grad = jnp.stack([gate_grad, up_grad], axis=1).astype(jnp.bfloat16)
    return act_grad, jnp.swapaxes(partial.reshape(2, 8, WIDTH), 0, 1)


def solution(mesh):
    placed = (
        P(("group", "blk"), None),
        P(("group", "blk"), None, None),
        P("blk", None, None),
        P(("group", "blk")),
        P(("group", "blk")),
    )
    return jax.shard_map(
        body,
        mesh=mesh,
        in_specs=placed,
        out_specs=(P(("group", "blk"), None, None), P(("group", "blk"), None, None)),
        check_vma=False,
    )
```

```python
import functools

import jax
import jax.numpy as jnp
from jax import lax
from jax.experimental import pallas as pl
from jax.experimental.pallas import tpu as pltpu
from jax.sharding import PartitionSpec as P

MESH = pl.DeviceIdType.MESH
grad_factor = 0.015625

ROWS = 768
HIDDEN = 1024
WIDTH = 3584
WIDE = 512
CHUNKS = WIDTH // WIDE
SPLIT = (384, 128)
STREAM_ROWS = (256, 64)
f32 = jnp.float32
bf16 = jnp.bfloat16

EVENTS = {1: ((1, 0), (2, 1)), 2: ((1, 1), (2, 0)), 3: ((4, 0), (4, 1)), 4: ((3, 0), (3, 1)),
          6: ((5, 0), (6, 1)), 7: ((5, 1), (6, 0)), 9: ((7, 0), (7, 1))}
ORDER = (0, 1, 2, 4, 3, 5, 6, 7)
TURNS = {2: (0,), 3: (1,), 4: (2,), 5: (3,), 6: (4,), 8: (5,), 9: (6,), 11: (7,)}


def kernel(
    cot_hbm, pre_hbm, w_hbm, expert_ref, fill_ref,
    act_hbm, wgrad_hbm,
    cot_own, cot_sib, pre, lhs, lhs_sib, w_all, grad_buf, out_buf, mixed,
    rings, tot,
    cot_sem, pre_sem, w_sem, grad_sem, out_sem,
    cs_send, cs_recv, ls_send, ls_recv,
    ag_send, ag_recv, sib_send, sib_recv,
):
    g = lax.axis_index("group")
    b = lax.axis_index("blk")
    x_lo, z = lax.div(g, 4), lax.rem(g, 4)
    y, c = lax.div(b, 4), lax.rem(b, 2)
    x_hi = lax.rem(lax.div(b, 2), 2)
    x = x_hi * 2 + x_lo

    def device(dx, dy, dz, core):
        xx, yy, zz = lax.rem(x + dx, 4), lax.rem(y + dy, 4), lax.rem(z + dz, 4)
        return (lax.rem(xx, 2) * 4 + zz, yy * 4 + lax.div(xx, 2) * 2 + core)

    other = 1 - c
    sibling = device(0, 0, 0, other)
    x_up, x_dn = device(1, 0, 0, c), device(3, 0, 0, c)
    y_up, y_dn = device(0, 1, 0, c), device(0, 3, 0, c)
    z_up, z_dn = device(0, 0, 1, c), device(0, 0, 3, c)
    x_peer = device(3 - 2 * x + 4, 0, 0, c)

    barrier = pltpu.get_barrier_semaphore()
    for peer in (sibling, x_up, x_dn, y_up, y_dn, z_up, z_dn):
        pl.semaphore_signal(barrier, inc=1, device_id=peer, device_id_type=MESH)

    def cot_cols(k):
        return pl.ds(pl.multiple_of(k * WIDE, WIDE), WIDE)

    def cot_copy(k):
        return pltpu.make_async_copy(cot_hbm.at[:, cot_cols(k)], cot_own.at[:, cot_cols(k)], cot_sem.at[k])

    def pre_copy():
        return pltpu.make_async_copy(pre_hbm, pre, pre_sem)

    q_own = y * 2 + x_hi

    def w_copy(e):
        return pltpu.make_async_copy(w_hbm.at[e], w_all.at[q_own, e, c], w_sem.at[e])

    for e in range(2):
        w_copy(e).start()
    pre_copy().start()

    @pl.loop(0, CHUNKS)
    def _(k):
        cot_copy(k).start()

    pl.semaphore_wait(barrier, 7)

    def remote(src, dst, send, recv, device_id):
        return pltpu.make_async_remote_copy(
            src_ref=src, dst_ref=dst, send_sem=send, recv_sem=recv, device_id=device_id, device_id_type=MESH
        )

    def lhs_remote():
        return remote(lhs.at[1], lhs_sib, ls_send, ls_recv, sibling)

    def cot_remote(k):
        return remote(
            cot_hbm.at[:, cot_cols(k)], cot_sib.at[:, cot_cols(k)], cs_send.at[k], cs_recv.at[k], sibling
        )

    def piece(j):
        yy = lax.rem(y + (0, 3, 1, 2)[j % 4], 4)
        return yy * 2 + (x_hi if j < 4 else 1 - x_hi)

    def gather(slot):
        src_j, dst_j, e, device_id = sends[slot]
        block = w_all.at[piece(src_j), e, c]
        return remote(block, block, ag_send.at[slot], ag_recv.at[dst_j, e], device_id)

    def gather_wait(j, e):
        block = w_all.at[piece(j), e, c]
        remote(block, block, ag_send.at[0], ag_recv.at[j, e], sibling).wait_recv()

    def share(j, e):
        block = w_all.at[piece(j), e, c]
        return remote(block, block, sib_send.at[j, e], sib_recv.at[j, e], sibling)

    def share_wait(j, e):
        block = w_all.at[piece(j), e, other]
        remote(block, block, sib_send.at[j, e], sib_recv.at[j, e], sibling).wait_recv()

    sends = [(0, 1, 0, y_up), (0, 2, 1, y_dn), (0, 4, 0, x_peer), (0, 4, 1, x_peer), (0, 1, 1, y_up), (0, 2, 0, y_dn)]
    sends += [(1, 3, 0, y_up), (2, 3, 1, y_dn)]
    for e in range(2):
        sends += [(4, 5, e, y_up), (4, 6, e, y_dn)]
    sends += [(5, 7, 0, y_up), (6, 7, 1, y_dn)]

    def gather_start(j, e):
        for slot, (src_j, _, src_e, _) in enumerate(sends):
            if (src_j, src_e) == (j, e):
                gather(slot).start()

    def arrived(j, e):
        gather_wait(j, e)
        gather_start(j, e)
        share(j, e).start()

    cot_remote(0).start()
    for e in range(2):
        w_copy(e).wait()
    for slot in range(6):
        gather(slot).start()

    @pl.loop(1, CHUNKS)
    def _(k):
        cot_remote(k).start()

    pre_copy().wait()

    @pl.loop(0, ROWS // 128)
    def _(t):
        rows = pl.ds(pl.multiple_of(t * 128, 128), 128)
        lane = lax.broadcasted_iota(jnp.int32, (8, 128), 1)
        alive = lane < fill_ref[t]
        chosen = jnp.zeros((8, 128), jnp.int32) + expert_ref[t]
        masks = [jnp.logical_and(alive, chosen == e) for e in range(2)]

        @pl.loop(0, 8)
        def _(part):
            cols = pl.ds(pl.multiple_of(part * 128, 128), 128)
            gate = pre[0, rows, cols].astype(f32)
            up = pre[1, rows, cols].astype(f32)
            sig = 1.0 / (1.0 + jnp.exp(-gate))
            turned = jnp.transpose(gate * sig * up)
            part_x, part_z = lax.div(part, 4), lax.rem(part, 4)
            for yy in range(4):
                for hi in range(2):
                    for core in range(2):
                        at = yy * 32 + hi * 16 + core * 8
                        value = turned[at:at + 8]
                        pair = jnp.concatenate([jnp.where(mask, value, 0.0) for mask in masks], axis=0)
                        lhs[lax.rem(c + core, 2), part_z, hi * 2 + part_x, yy * 16:yy * 16 + 16, rows] = pair.astype(bf16)

    lhs_remote().start()
    for e in range(2):
        share(0, e).start()

    z_ring, x_ring, y_ring = (z, z_up, z_dn), (x, x_up, x_dn), (y, y_up, y_dn)
    ring_of = ((z_ring, x_ring), (x_ring, z_ring), (y_ring,))

    def far_copy(st, s, k, half):
        far, rfar, send, recv = (rings[st][s][i] for i in (0, 3, 8, 9))
        rows = far.shape[1] // 2
        return remote(
            far.at[k, pl.ds(half * rows, rows)], rfar.at[k, pl.ds(half * rows, rows)],
            send.at[k, half], recv.at[k, half], ring_of[st][s][1 + half],
        )

    def near_copy(st, s, k, way):
        src, dst, send, recv = (rings[st][s][i] for i in (1 + way, 4 + way, 8, 9))
        return remote(src.at[k], dst.at[k], send.at[k, 2 + way], recv.at[k, 2 + way], ring_of[st][s][1 + way])

    def emit(st, s, k, offset, value):
        far, up, dn, _, _, _, own, rel, _, _ = rings[st][s]
        half = far.shape[1] // 2
        kind = far.dtype
        if offset == 2:
            far[k] = value.astype(kind)
            far_copy(st, s, k, 0).start()
            far_copy(st, s, k, 1).start()
        elif offset == 1:
            rel[lax.rem(k, 2), 0] = value[:half]
            up[k, half:] = value[half:].astype(kind)
        elif offset == 3:
            rel[lax.rem(k, 2), 1] = value[half:]
            dn[k, :half] = value[:half].astype(kind)
        else:
            own[lax.rem(k, 4)] = value

    def relay(st, s, k):
        _, up, dn, rfar, _, _, _, rel, _, _ = rings[st][s]
        half = up.shape[1] // 2
        kind = up.dtype
        far_copy(st, s, k, 0).wait_recv()
        up[k, :half] = (rel[lax.rem(k, 2), 0] + rfar[k, :half].astype(f32)).astype(kind)
        near_copy(st, s, k, 0).start()
        far_copy(st, s, k, 1).wait_recv()
        dn[k, half:] = (rel[lax.rem(k, 2), 1] + rfar[k, half:].astype(f32)).astype(kind)
        near_copy(st, s, k, 1).start()

    def total(st, s, k):
        near_copy(st, s, k, 0).wait_recv()
        near_copy(st, s, k, 1).wait_recv()
        _, _, _, _, rup, rdn, own, _, _, _ = rings[st][s]
        return own[lax.rem(k, 4)] + rup[k].astype(f32) + rdn[k].astype(f32)

    def make(k):
        cot_remote(k).wait_recv()
        cols = cot_cols(k)
        for offset in (2, 1, 3, 0):
            at = lax.rem(z + offset, 4)
            value = jnp.dot(lhs[0, at].reshape(256, ROWS), cot_own[:, cols], preferred_element_type=f32)
            value += jnp.dot(lhs_sib[at].reshape(256, ROWS), cot_sib[:, cols], preferred_element_type=f32)
            emit(0, 0, k, offset, value[:, :SPLIT[0]])
            mixed[at] = value[:, SPLIT[0]:].reshape(4, 64, SPLIT[1])
        for offset in (2, 1, 3, 0):
            at = lax.rem(x + offset, 4)
            emit(1, 0, k, offset, mixed[:, at].reshape(256, SPLIT[1]))

    def onward(k):
        for st in range(2):
            tot[st][...] = total(st, 0, k)
            me = ring_of[st][1][0]
            for offset in (2, 1, 3, 0):
                at = pl.multiple_of(lax.rem(me + offset, 4) * 64, 64)
                emit(st, 1, k, offset, tot[st][pl.ds(at, 64), :])

    def joined(k):
        for st in range(2):
            tot[2][:, st * SPLIT[0]:st * SPLIT[0] + SPLIT[st]] = total(st, 1, k)
        for offset in (2, 1, 3, 0):
            at = pl.multiple_of(lax.rem(y + offset, 4) * 16, 16)
            emit(2, 0, k, offset, tot[2][pl.ds(at, 16), :])

    def last(k):
        out_buf[:, cot_cols(k)] = total(2, 0, k) * grad_factor

    def grad_copy(turn):
        cols = pl.ds(pl.multiple_of(piece(ORDER[turn]) * 128, 128), 128)
        return pltpu.make_async_copy(grad_buf.at[turn % 2], act_hbm.at[:, :, cols], grad_sem.at[turn])

    def hidden(turn):
        j = ORDER[turn]
        for e in range(2):
            share_wait(j, e)
        if turn >= 2:
            grad_copy(turn - 2).wait()
        q = piece(j)
        cols = pl.ds(pl.multiple_of(q * 128, 128), 128)

        @pl.loop(0, ROWS // 256)
        def _(m):
            rows = pl.ds(pl.multiple_of(m * 256, 256), 256)
            each = lax.dot_general(
                cot_own[rows, :], w_all[q].reshape(256, WIDTH), (((1,), (1,)), ((), ())), preferred_element_type=f32
            )
            for i in range(2):
                part = pl.ds(pl.multiple_of(m * 256 + i * 128, 128), 128)
                row = lax.broadcasted_iota(jnp.int32, (128, 128), 0)
                alive = row < fill_ref[m * 2 + i]
                second = jnp.zeros((128, 128), jnp.int32) + expert_ref[m * 2 + i] == 1
                both = each[i * 128:(i + 1) * 128]
                grad = jnp.where(alive, jnp.where(second, both[:, 128:], both[:, :128]), 0.0)
                gate = pre[0, part, cols].astype(f32)
                up = pre[1, part, cols].astype(f32)
                sig = 1.0 / (1.0 + jnp.exp(-gate))
                grad_buf[turn % 2, 0, part, :] = (grad * up * sig * (1.0 + gate * (1.0 - sig))).astype(bf16)
                grad_buf[turn % 2, 1, part, :] = (grad * (gate * sig)).astype(bf16)

        grad_copy(turn).start()

    @pl.loop(0, CHUNKS)
    def _(k):
        cot_copy(k).wait()

    lhs_remote().wait_recv()

    @pl.loop(0, CHUNKS + 6)
    def _(t):
        def at(lag, do):
            @pl.when(jnp.logical_and(t >= lag, t < CHUNKS + lag))
            def _():
                do(t - lag)

        def on(when, do):
            @pl.when(t == when)
            def _():
                do()

        def both(do, s):
            def run(k):
                for st in range(2):
                    do(st, s, k)

            return run

        for when, those in EVENTS.items():
            for j, e in those:
                on(when, functools.partial(arrived, j, e))
        at(0, make)
        at(1, both(relay, 0))
        at(2, onward)
        at(3, both(relay, 1))
        at(4, joined)
        at(5, functools.partial(relay, 2, 0))
        at(6, last)

        for when, those in TURNS.items():
            for turn in those:
                on(when, functools.partial(hidden, turn))

    out = pltpu.make_async_copy(out_buf, wgrad_hbm, out_sem)
    out.start()
    for turn in (6, 7):
        grad_copy(turn).wait()
    out.wait()

    lhs_remote().wait_send()

    @pl.loop(0, CHUNKS)
    def _(k):
        cot_remote(k).wait_send()
        for st, s in ((0, 0), (0, 1), (1, 0), (1, 1), (2, 0)):
            for i in range(2):
                far_copy(st, s, k, i).wait_send()
                near_copy(st, s, k, i).wait_send()

    for slot in range(len(sends)):
        gather(slot).wait_send()
    for j in range(8):
        for e in range(2):
            share(j, e).wait_send()


def ring_scratch(rows, cols, kind):
    dma = pltpu.SemaphoreType.DMA
    return (
        *[pltpu.VMEM((CHUNKS, rows, cols), kind)] * 6,
        pltpu.VMEM((4, rows, cols), f32),
        pltpu.VMEM((2, 2, rows // 2, cols), f32),
        dma((CHUNKS, 4)),
        dma((CHUNKS, 4)),
    )


def call(cot, pre, w, expert, fill):
    dma = pltpu.SemaphoreType.DMA
    any_space = pl.BlockSpec(memory_space=pl.ANY)
    scalars = pl.BlockSpec(memory_space=pltpu.SMEM)
    return pl.pallas_call(
        kernel,
        out_shape=(
            jax.ShapeDtypeStruct((2, ROWS, HIDDEN), bf16),
            jax.ShapeDtypeStruct((16, WIDTH), f32),
        ),
        in_specs=[any_space, any_space, any_space, scalars, scalars],
        out_specs=(any_space, any_space),
        scratch_shapes=[
            pltpu.VMEM((ROWS, WIDTH), bf16),
            pltpu.VMEM((ROWS, WIDTH), bf16),
            pltpu.VMEM((2, ROWS, HIDDEN), bf16),
            pltpu.VMEM((2, 4, 4, 64, ROWS), bf16),
            pltpu.VMEM((4, 4, 64, ROWS), bf16),
            pltpu.VMEM((8, 2, 2, 64, WIDTH), bf16),
            pltpu.VMEM((2, 2, ROWS, 128), bf16),
            pltpu.VMEM((16, WIDTH), f32),
            pltpu.VMEM((4, 4, 64, SPLIT[1]), f32),
            (
                tuple(ring_scratch(r, SPLIT[0], bf16) for r in STREAM_ROWS),
                tuple(ring_scratch(r, SPLIT[1], bf16) for r in STREAM_ROWS),
                (ring_scratch(16, WIDE, f32),),
            ),
            (pltpu.VMEM((256, SPLIT[0]), f32), pltpu.VMEM((256, SPLIT[1]), f32), pltpu.VMEM((64, WIDE), f32)),
            dma((CHUNKS,)), dma, dma((2,)), dma((8,)), dma,
            dma((CHUNKS,)), dma((CHUNKS,)), dma, dma,
            dma((14,)), dma((8, 2)), dma((8, 2)), dma((8, 2)),
        ],
        compiler_params=pltpu.CompilerParams(
            collective_id=0, has_side_effects=True, vmem_limit_bytes=60 * 2**20
        ),
        cost_estimate=pl.CostEstimate(flops=24 * 10**9, bytes_accessed=30 * 10**6, transcendentals=0),
    )(cot, pre, w, expert, fill)


def body(cotangent, pre_act, down_weight, tile_expert, tile_fill):
    act_grad, partial = call(
        cotangent, jnp.swapaxes(pre_act, 0, 1), jnp.swapaxes(down_weight, 0, 1), tile_expert, tile_fill
    )
    return jnp.swapaxes(act_grad, 0, 1), jnp.swapaxes(partial.reshape(2, 8, WIDTH), 0, 1)


def solution(mesh):
    placed = (
        P(("group", "blk"), None),
        P(("group", "blk"), None, None),
        P("blk", None, None),
        P(("group", "blk")),
        P(("group", "blk")),
    )
    return jax.shard_map(
        body,
        mesh=mesh,
        in_specs=placed,
        out_specs=(P(("group", "blk"), None, None), P(("group", "blk"), None, None)),
        check_vma=False,
    )
```

```python
import functools

import jax
import jax.numpy as jnp
from jax import lax
from jax.experimental import pallas as pl
from jax.experimental.pallas import tpu as pltpu
from jax.sharding import PartitionSpec as P

MESH = pl.DeviceIdType.MESH
grad_factor = 0.015625

ROWS = 768
HIDDEN = 1024
WIDTH = 3584
WIDE = 512
CHUNKS = WIDTH // WIDE
SPLIT = (384, 128)
f32 = jnp.float32
bf16 = jnp.bfloat16

EVENTS = {1: ((1, 0), (2, 1)), 2: ((1, 1), (2, 0), (4, 0), (4, 1)), 4: ((3, 0), (3, 1)),
          5: ((5, 0), (6, 1)), 7: ((5, 1), (6, 0)), 10: ((7, 0), (7, 1))}
ORDER = (0, 1, 2, 4, 3, 5, 6, 7)
TURNS = {2: (0,), 3: (1,), 4: (2,), 5: (3,), 6: (4,), 8: (5,), 9: (6,), 10: (7,)}


def kernel(
    cot_hbm, pre_hbm, w_hbm, expert_ref, fill_ref,
    act_hbm, wgrad_hbm,
    cot_own, cot_sib, pre, lhs, lhs_sib, w_all, grad_buf, out_buf, mixed,
    rings, directs, tot,
    cot_sem, pre_sem, w_sem, grad_sem, out_sem,
    cs_send, cs_recv, ls_send, ls_recv,
    ag_send, ag_recv, sib_send, sib_recv,
):
    g = lax.axis_index("group")
    b = lax.axis_index("blk")
    x_lo, z = lax.div(g, 4), lax.rem(g, 4)
    y, c = lax.div(b, 4), lax.rem(b, 2)
    x_hi = lax.rem(lax.div(b, 2), 2)
    x = x_hi * 2 + x_lo

    def device(dx, dy, dz, core):
        xx, yy, zz = lax.rem(x + dx, 4), lax.rem(y + dy, 4), lax.rem(z + dz, 4)
        return (lax.rem(xx, 2) * 4 + zz, yy * 4 + lax.div(xx, 2) * 2 + core)

    other = 1 - c
    sibling = device(0, 0, 0, other)
    x_up, x_dn = device(1, 0, 0, c), device(3, 0, 0, c)
    y_up, y_dn = device(0, 1, 0, c), device(0, 3, 0, c)
    z_up, z_dn = device(0, 0, 1, c), device(0, 0, 3, c)
    x_far, y_far, z_far = device(2, 0, 0, c), device(0, 2, 0, c), device(0, 0, 2, c)
    x_peer = device(3 - 2 * x + 4, 0, 0, c)

    barrier = pltpu.get_barrier_semaphore()
    for peer in (sibling, x_up, x_dn, x_far, y_up, y_dn, y_far, z_up, z_dn, z_far):
        pl.semaphore_signal(barrier, inc=1, device_id=peer, device_id_type=MESH)

    def cot_cols(k):
        return pl.ds(pl.multiple_of(k * WIDE, WIDE), WIDE)

    def cot_copy(k):
        return pltpu.make_async_copy(cot_hbm.at[:, cot_cols(k)], cot_own.at[:, cot_cols(k)], cot_sem.at[k])

    def pre_copy():
        return pltpu.make_async_copy(pre_hbm, pre, pre_sem)

    q_own = y * 2 + x_hi

    def w_copy(e):
        return pltpu.make_async_copy(w_hbm.at[e], w_all.at[q_own, e, c], w_sem.at[e])

    for e in range(2):
        w_copy(e).start()
    pre_copy().start()

    @pl.loop(0, CHUNKS)
    def _(k):
        cot_copy(k).start()

    pl.semaphore_wait(barrier, 10)

    def remote(src, dst, send, recv, device_id):
        return pltpu.make_async_remote_copy(
            src_ref=src, dst_ref=dst, send_sem=send, recv_sem=recv, device_id=device_id, device_id_type=MESH
        )

    def lhs_remote(t):
        rows = pl.ds(pl.multiple_of(t * 128, 128), 128)
        return remote(
            lhs.at[1, :, :, :, rows], lhs_sib.at[:, :, :, rows], ls_send.at[t], ls_recv.at[t], sibling
        )

    def cot_remote(k):
        return remote(
            cot_hbm.at[:, cot_cols(k)], cot_sib.at[:, cot_cols(k)], cs_send.at[k], cs_recv.at[k], sibling
        )

    def piece(j):
        yy = lax.rem(y + (0, 3, 1, 2)[j % 4], 4)
        return yy * 2 + (x_hi if j < 4 else 1 - x_hi)

    def gather(slot):
        src_j, dst_j, e, device_id = sends[slot]
        block = w_all.at[piece(src_j), e, c]
        return remote(block, block, ag_send.at[slot], ag_recv.at[dst_j, e], device_id)

    def gather_wait(j, e):
        block = w_all.at[piece(j), e, c]
        remote(block, block, ag_send.at[0], ag_recv.at[j, e], sibling).wait_recv()

    def share(j, e):
        block = w_all.at[piece(j), e, c]
        return remote(block, block, sib_send.at[j, e], sib_recv.at[j, e], sibling)

    def share_wait(j, e):
        block = w_all.at[piece(j), e, other]
        remote(block, block, sib_send.at[j, e], sib_recv.at[j, e], sibling).wait_recv()

    sends = [(0, 1, 0, y_up), (0, 2, 1, y_dn), (0, 4, 0, x_peer), (0, 4, 1, x_peer), (0, 1, 1, y_up), (0, 2, 0, y_dn)]
    sends += [(1, 3, 0, y_up), (2, 3, 1, y_dn)]
    for e in range(2):
        sends += [(4, 5, e, y_up), (4, 6, e, y_dn)]
    sends += [(5, 7, 0, y_up), (6, 7, 1, y_dn)]

    def gather_start(j, e):
        for slot, (src_j, _, src_e, _) in enumerate(sends):
            if (src_j, src_e) == (j, e):
                gather(slot).start()

    def arrived(j, e):
        gather_wait(j, e)
        gather_start(j, e)
        share(j, e).start()

    cot_remote(0).start()
    for e in range(2):
        w_copy(e).wait()
    for slot in range(6):
        gather(slot).start()

    pre_copy().wait()

    @pl.loop(0, ROWS // 128)
    def _(t):
        rows = pl.ds(pl.multiple_of(t * 128, 128), 128)
        lane = lax.broadcasted_iota(jnp.int32, (8, 128), 1)
        alive = lane < fill_ref[t]
        chosen = jnp.zeros((8, 128), jnp.int32) + expert_ref[t]
        masks = [jnp.logical_and(alive, chosen == e) for e in range(2)]

        @pl.loop(0, 8)
        def _(part):
            cols = pl.ds(pl.multiple_of(part * 128, 128), 128)
            gate = pre[0, rows, cols].astype(f32)
            up = pre[1, rows, cols].astype(f32)
            sig = 1.0 / (1.0 + jnp.exp(-gate))
            turned = jnp.transpose(gate * sig * up)
            part_x, part_z = lax.div(part, 4), lax.rem(part, 4)
            for yy in range(4):
                for hi in range(2):
                    for core in range(2):
                        at = yy * 32 + hi * 16 + core * 8
                        value = turned[at:at + 8]
                        pair = jnp.concatenate([jnp.where(mask, value, 0.0) for mask in masks], axis=0)
                        lhs[lax.rem(c + core, 2), part_z, hi * 2 + part_x, yy * 16:yy * 16 + 16, rows] = pair.astype(bf16)

        lhs_remote(t).start()

    @pl.loop(1, CHUNKS)
    def _(k):
        cot_remote(k).start()

    for e in range(2):
        share(0, e).start()

    z_ring, x_ring, y_ring = (z, z_up, z_dn, z_far), (x, x_up, x_dn, x_far), (y, y_up, y_dn, y_far)
    ring_of = (z_ring, x_ring)
    direct_of = (x_ring, z_ring, y_ring)

    def far_copy(st, k, half):
        far, rfar, send, recv = (rings[st][i] for i in (0, 3, 8, 9))
        rows = far.shape[1] // 2
        return remote(
            far.at[k, pl.ds(half * rows, rows)], rfar.at[k, pl.ds(half * rows, rows)],
            send.at[k, half], recv.at[k, half], ring_of[st][1 + half],
        )

    def near_copy(st, k, way):
        src, dst, send, recv = (rings[st][i] for i in (1 + way, 4 + way, 8, 9))
        return remote(src.at[k], dst.at[k], send.at[k, 2 + way], recv.at[k, 2 + way], ring_of[st][1 + way])

    def emit(st, k, offset, value):
        far, up, dn, _, _, _, own, rel, _, _ = rings[st]
        half = far.shape[1] // 2
        kind = far.dtype
        if offset == 2:
            far[k] = value.astype(kind)
            far_copy(st, k, 0).start()
            far_copy(st, k, 1).start()
        elif offset == 1:
            rel[lax.rem(k, 2), 0] = value[:half]
            up[k, half:] = value[half:].astype(kind)
        elif offset == 3:
            rel[lax.rem(k, 2), 1] = value[half:]
            dn[k, :half] = value[:half].astype(kind)
        else:
            own[lax.rem(k, 4)] = value

    def relay(k):
        for st in range(2):
            _, up, dn, rfar, _, _, _, rel, _, _ = rings[st]
            half = up.shape[1] // 2
            kind = up.dtype
            far_copy(st, k, 0).wait_recv()
            up[k, :half] = (rel[lax.rem(k, 2), 0] + rfar[k, :half].astype(f32)).astype(kind)
            near_copy(st, k, 0).start()
            far_copy(st, k, 1).wait_recv()
            dn[k, half:] = (rel[lax.rem(k, 2), 1] + rfar[k, half:].astype(f32)).astype(kind)
            near_copy(st, k, 1).start()

    def total(st, k):
        near_copy(st, k, 0).wait_recv()
        near_copy(st, k, 1).wait_recv()
        _, _, _, _, rup, rdn, own, _, _, _ = rings[st]
        return own[lax.rem(k, 4)] + rup[k].astype(f32) + rdn[k].astype(f32)

    def direct_copy(st, k, i):
        out, came, _, send, recv = directs[st]
        return remote(out.at[k, i], came.at[k, i], send.at[k, i], recv.at[k, i], direct_of[st][1 + i])

    def spread(st, k, load):
        out, _, own, _, _ = directs[st]
        for i, offset in ((2, 2), (0, 1), (1, 3)):
            out[k, i] = load(lax.rem(direct_of[st][0] + offset, 4)).astype(out.dtype)
            direct_copy(st, k, i).start()
        own[lax.rem(k, 2)] = load(direct_of[st][0])

    def collected(st, k):
        _, came, own, _, _ = directs[st]
        for i in range(3):
            direct_copy(st, k, i).wait_recv()
        return own[lax.rem(k, 2)] + came[k, 0].astype(f32) + came[k, 1].astype(f32) + came[k, 2].astype(f32)

    def make(k):
        cot_remote(k).wait_recv()
        cols = cot_cols(k)
        for offset in (2, 1, 3, 0):
            at = lax.rem(z + offset, 4)
            value = jnp.dot(lhs[0, at].reshape(256, ROWS), cot_own[:, cols], preferred_element_type=f32)
            value += jnp.dot(lhs_sib[at].reshape(256, ROWS), cot_sib[:, cols], preferred_element_type=f32)
            emit(0, k, offset, value[:, :SPLIT[0]])
            mixed[at] = value[:, SPLIT[0]:].reshape(4, 64, SPLIT[1])
        for offset in (2, 1, 3, 0):
            at = lax.rem(x + offset, 4)
            emit(1, k, offset, mixed[:, at].reshape(256, SPLIT[1]))

    def onward(k):
        for st in range(2):
            tot[st][...] = total(st, k)
            spread(st, k, lambda at: tot[st][pl.ds(pl.multiple_of(at * 64, 64), 64), :])

    def joined(k):
        for st in range(2):
            tot[2][:, st * SPLIT[0]:st * SPLIT[0] + SPLIT[st]] = collected(st, k)
        spread(2, k, lambda at: tot[2][pl.ds(pl.multiple_of(at * 16, 16), 16), :])

    def last(k):
        out_buf[:, cot_cols(k)] = collected(2, k) * grad_factor

    def grad_copy(turn):
        cols = pl.ds(pl.multiple_of(piece(ORDER[turn]) * 128, 128), 128)
        return pltpu.make_async_copy(grad_buf.at[turn % 2], act_hbm.at[:, :, cols], grad_sem.at[turn])

    def hidden(turn):
        j = ORDER[turn]
        for e in range(2):
            share_wait(j, e)
        if turn >= 2:
            grad_copy(turn - 2).wait()
        q = piece(j)
        cols = pl.ds(pl.multiple_of(q * 128, 128), 128)

        @pl.loop(0, ROWS // 256)
        def _(m):
            rows = pl.ds(pl.multiple_of(m * 256, 256), 256)
            each = lax.dot_general(
                cot_own[rows, :], w_all[q].reshape(256, WIDTH), (((1,), (1,)), ((), ())), preferred_element_type=f32
            )
            for i in range(2):
                part = pl.ds(pl.multiple_of(m * 256 + i * 128, 128), 128)
                row = lax.broadcasted_iota(jnp.int32, (128, 128), 0)
                alive = row < fill_ref[m * 2 + i]
                second = jnp.zeros((128, 128), jnp.int32) + expert_ref[m * 2 + i] == 1
                both = each[i * 128:(i + 1) * 128]
                grad = jnp.where(alive, jnp.where(second, both[:, 128:], both[:, :128]), 0.0)
                gate = pre[0, part, cols].astype(f32)
                up = pre[1, part, cols].astype(f32)
                sig = 1.0 / (1.0 + jnp.exp(-gate))
                grad_buf[turn % 2, part, 0, :] = (grad * up * sig * (1.0 + gate * (1.0 - sig))).astype(bf16)
                grad_buf[turn % 2, part, 1, :] = (grad * (gate * sig)).astype(bf16)

        grad_copy(turn).start()

    @pl.loop(0, CHUNKS)
    def _(k):
        cot_copy(k).wait()

    @pl.loop(0, ROWS // 128)
    def _(t):
        lhs_remote(t).wait_recv()

    @pl.loop(0, CHUNKS + 4)
    def _(t):
        def at(lag, do):
            @pl.when(jnp.logical_and(t >= lag, t < CHUNKS + lag))
            def _():
                do(t - lag)

        def on(when, do):
            @pl.when(t == when)
            def _():
                do()

        for when, those in EVENTS.items():
            for j, e in those:
                on(when, functools.partial(arrived, j, e))
        at(0, make)
        at(1, relay)
        at(2, onward)
        at(3, joined)
        at(4, last)

        for when, those in TURNS.items():
            for turn in those:
                on(when, functools.partial(hidden, turn))

    out = pltpu.make_async_copy(out_buf, wgrad_hbm, out_sem)
    out.start()
    for turn in (6, 7):
        grad_copy(turn).wait()
    out.wait()

    @pl.loop(0, ROWS // 128)
    def _(t):
        lhs_remote(t).wait_send()

    @pl.loop(0, CHUNKS)
    def _(k):
        cot_remote(k).wait_send()
        for st in range(2):
            for i in range(2):
                far_copy(st, k, i).wait_send()
                near_copy(st, k, i).wait_send()
        for st in range(3):
            for i in range(3):
                direct_copy(st, k, i).wait_send()

    for slot in range(len(sends)):
        gather(slot).wait_send()
    for j in range(8):
        for e in range(2):
            share(j, e).wait_send()


def ring_scratch(rows, cols, kind):
    dma = pltpu.SemaphoreType.DMA
    return (
        *[pltpu.VMEM((CHUNKS, rows, cols), kind)] * 6,
        pltpu.VMEM((4, rows, cols), f32),
        pltpu.VMEM((2, 2, rows // 2, cols), f32),
        dma((CHUNKS, 4)),
        dma((CHUNKS, 4)),
    )


def direct_scratch(rows, cols, kind):
    dma = pltpu.SemaphoreType.DMA
    return (
        pltpu.VMEM((CHUNKS, 3, rows, cols), kind),
        pltpu.VMEM((CHUNKS, 3, rows, cols), kind),
        pltpu.VMEM((2, rows, cols), f32),
        dma((CHUNKS, 3)),
        dma((CHUNKS, 3)),
    )


def call(cot, pre, w, expert, fill):
    dma = pltpu.SemaphoreType.DMA
    any_space = pl.BlockSpec(memory_space=pl.ANY)
    scalars = pl.BlockSpec(memory_space=pltpu.SMEM)
    return pl.pallas_call(
        kernel,
        out_shape=(
            jax.ShapeDtypeStruct((ROWS, 2, HIDDEN), bf16),
            jax.ShapeDtypeStruct((16, WIDTH), f32),
        ),
        in_specs=[any_space, any_space, any_space, scalars, scalars],
        out_specs=(any_space, any_space),
        scratch_shapes=[
            pltpu.VMEM((ROWS, WIDTH), bf16),
            pltpu.VMEM((ROWS, WIDTH), bf16),
            pltpu.VMEM((2, ROWS, HIDDEN), bf16),
            pltpu.VMEM((2, 4, 4, 64, ROWS), bf16),
            pltpu.VMEM((4, 4, 64, ROWS), bf16),
            pltpu.VMEM((8, 2, 2, 64, WIDTH), bf16),
            pltpu.VMEM((2, ROWS, 2, 128), bf16),
            pltpu.VMEM((16, WIDTH), f32),
            pltpu.VMEM((4, 4, 64, SPLIT[1]), f32),
            tuple(ring_scratch(256, cols, bf16) for cols in SPLIT),
            (
                direct_scratch(64, SPLIT[0], bf16),
                direct_scratch(64, SPLIT[1], bf16),
                direct_scratch(16, WIDE, f32),
            ),
            (pltpu.VMEM((256, SPLIT[0]), f32), pltpu.VMEM((256, SPLIT[1]), f32), pltpu.VMEM((64, WIDE), f32)),
            dma((CHUNKS,)), dma, dma((2,)), dma((8,)), dma,
            dma((CHUNKS,)), dma((CHUNKS,)), dma((6,)), dma((6,)),
            dma((14,)), dma((8, 2)), dma((8, 2)), dma((8, 2)),
        ],
        compiler_params=pltpu.CompilerParams(
            collective_id=0, has_side_effects=True, vmem_limit_bytes=60 * 2**20
        ),
        cost_estimate=pl.CostEstimate(flops=24 * 10**9, bytes_accessed=30 * 10**6, transcendentals=0),
    )(cot, pre, w, expert, fill)


def body(cotangent, pre_act, down_weight, tile_expert, tile_fill):
    act_grad, partial = call(
        cotangent, jnp.swapaxes(pre_act, 0, 1), jnp.swapaxes(down_weight, 0, 1), tile_expert, tile_fill
    )
    return act_grad, jnp.swapaxes(partial.reshape(2, 8, WIDTH), 0, 1)


def solution(mesh):
    placed = (
        P(("group", "blk"), None),
        P(("group", "blk"), None, None),
        P("blk", None, None),
        P(("group", "blk")),
        P(("group", "blk")),
    )
    return jax.shard_map(
        body,
        mesh=mesh,
        in_specs=placed,
        out_specs=(P(("group", "blk"), None, None), P(("group", "blk"), None, None)),
        check_vma=False,
    )
```

```python
import functools

import jax
import jax.numpy as jnp
from jax import lax
from jax.experimental import pallas as pl
from jax.experimental.pallas import tpu as pltpu
from jax.sharding import PartitionSpec as P

MESH = pl.DeviceIdType.MESH
grad_factor = 0.015625

ROWS = 768
HIDDEN = 1024
WIDTH = 3584
WIDE = 512
CHUNKS = WIDTH // WIDE
SPLIT = (384, 128)
f32 = jnp.float32
bf16 = jnp.bfloat16

EVENTS = {1: ((1, 0), (2, 1), (4, 0)), 3: ((1, 1), (2, 0)), 4: ((4, 1), (3, 0), (3, 1)),
          6: ((5, 0), (6, 0)), 7: ((5, 1), (6, 1)), 10: ((7, 0), (7, 1))}
HOPS = (1, 2)
ORDER = (0, 1, 2, 4, 3, 5, 6, 7)
TURNS = {2: (0,), 3: (1,), 4: (2,), 5: (3,), 6: (4,), 8: (5,), 9: (6,), 10: (7,)}


def kernel(
    cot_hbm, pre_hbm, w_hbm, expert_ref, fill_ref,
    act_hbm, wgrad_hbm,
    cot_own, cot_sib, pre, lhs, lhs_sib, w_all, grad_buf, out_buf, mixed,
    rings, directs, tot,
    cot_sem, pre_sem, w_sem, grad_sem, out_sem,
    cs_send, cs_recv, ls_send, ls_recv,
    ag_send, ag_recv, sib_send, sib_recv, hop_send, hop_recv,
):
    g = lax.axis_index("group")
    b = lax.axis_index("blk")
    x_lo, z = lax.div(g, 4), lax.rem(g, 4)
    y, c = lax.div(b, 4), lax.rem(b, 2)
    x_hi = lax.rem(lax.div(b, 2), 2)
    x = x_hi * 2 + x_lo

    def device(dx, dy, dz, core):
        xx, yy, zz = lax.rem(x + dx, 4), lax.rem(y + dy, 4), lax.rem(z + dz, 4)
        return (lax.rem(xx, 2) * 4 + zz, yy * 4 + lax.div(xx, 2) * 2 + core)

    other = 1 - c
    sibling = device(0, 0, 0, other)
    x_up, x_dn = device(1, 0, 0, c), device(3, 0, 0, c)
    y_up, y_dn = device(0, 1, 0, c), device(0, 3, 0, c)
    z_up, z_dn = device(0, 0, 1, c), device(0, 0, 3, c)
    x_far, y_far, z_far = device(2, 0, 0, c), device(0, 2, 0, c), device(0, 0, 2, c)
    x_peer = device(3 - 2 * x + 4, 0, 0, c)

    barrier = pltpu.get_barrier_semaphore()
    for peer in (sibling, x_up, x_dn, x_far, y_up, y_dn, y_far, z_up, z_dn, z_far):
        pl.semaphore_signal(barrier, inc=1, device_id=peer, device_id_type=MESH)

    def cot_cols(k):
        return pl.ds(pl.multiple_of(k * WIDE, WIDE), WIDE)

    def cot_copy(k):
        return pltpu.make_async_copy(cot_hbm.at[:, cot_cols(k)], cot_own.at[:, cot_cols(k)], cot_sem.at[k])

    def pre_copy():
        return pltpu.make_async_copy(pre_hbm, pre, pre_sem)

    q_own = y * 2 + x_hi

    def w_copy(e):
        return pltpu.make_async_copy(w_hbm.at[e], w_all.at[q_own, e, c], w_sem.at[e])

    for e in range(2):
        w_copy(e).start()
    pre_copy().start()

    @pl.loop(0, CHUNKS)
    def _(k):
        cot_copy(k).start()

    pl.semaphore_wait(barrier, 10)

    def remote(src, dst, send, recv, device_id):
        return pltpu.make_async_remote_copy(
            src_ref=src, dst_ref=dst, send_sem=send, recv_sem=recv, device_id=device_id, device_id_type=MESH
        )

    def lhs_remote(t):
        rows = pl.ds(pl.multiple_of(t * 128, 128), 128)
        return remote(
            lhs.at[1, :, :, :, rows], lhs_sib.at[:, :, :, rows], ls_send.at[t], ls_recv.at[t], sibling
        )

    def cot_remote(k):
        return remote(
            cot_hbm.at[:, cot_cols(k)], cot_sib.at[:, cot_cols(k)], cs_send.at[k], cs_recv.at[k], sibling
        )

    def piece(j):
        yy = lax.rem(y + (0, 3, 1, 2)[j % 4], 4)
        return yy * 2 + (x_hi if j < 4 else 1 - x_hi)

    def gather(slot):
        src_j, dst_j, e, device_id = sends[slot]
        block = w_all.at[piece(src_j), e, c]
        return remote(block, block, ag_send.at[slot], ag_recv.at[dst_j, e], device_id)

    def hop(i):
        block = w_all.at[piece(0), 1, c, pl.ds(i * 32, 32)]
        return remote(block, block, hop_send.at[i], hop_recv.at[i], x_peer)

    def hop_wait(i):
        block = w_all.at[piece(4), 1, c, pl.ds(i * 32, 32)]
        remote(block, block, hop_send.at[i], hop_recv.at[i], x_peer).wait_recv()

    def gather_wait(j, e):
        if (j, e) == (4, 1):
            for i in range(2):
                hop_wait(i)
        else:
            block = w_all.at[piece(j), e, c]
            remote(block, block, ag_send.at[0], ag_recv.at[j, e], sibling).wait_recv()

    def share(j, e):
        block = w_all.at[piece(j), e, c]
        return remote(block, block, sib_send.at[j, e], sib_recv.at[j, e], sibling)

    def share_wait(j, e):
        block = w_all.at[piece(j), e, other]
        remote(block, block, sib_send.at[j, e], sib_recv.at[j, e], sibling).wait_recv()

    sends = [(0, 1, 0, y_up), (0, 2, 1, y_dn), (0, 4, 0, x_peer), (0, 1, 1, y_up), (0, 2, 0, y_dn)]
    sends += [(1, 3, 0, y_up), (2, 3, 1, y_dn)]
    for e in range(2):
        sends += [(4, 5, e, y_up), (4, 6, e, y_dn)]
    sends += [(5, 7, 0, y_up), (6, 7, 1, y_dn)]

    def gather_start(j, e):
        for slot, (src_j, _, src_e, _) in enumerate(sends):
            if (src_j, src_e) == (j, e):
                gather(slot).start()

    def arrived(j, e):
        gather_wait(j, e)
        gather_start(j, e)
        share(j, e).start()

    cot_remote(0).start()
    for e in range(2):
        w_copy(e).wait()
    for slot in range(5):
        gather(slot).start()

    pre_copy().wait()

    @pl.loop(0, ROWS // 128)
    def _(t):
        rows = pl.ds(pl.multiple_of(t * 128, 128), 128)
        lane = lax.broadcasted_iota(jnp.int32, (8, 128), 1)
        alive = lane < fill_ref[t]
        chosen = jnp.zeros((8, 128), jnp.int32) + expert_ref[t]
        masks = [jnp.logical_and(alive, chosen == e) for e in range(2)]

        @pl.loop(0, 8)
        def _(part):
            cols = pl.ds(pl.multiple_of(part * 128, 128), 128)
            gate = pre[0, rows, cols].astype(f32)
            up = pre[1, rows, cols].astype(f32)
            sig = 1.0 / (1.0 + jnp.exp(-gate))
            turned = jnp.transpose(gate * sig * up)
            part_x, part_z = lax.div(part, 4), lax.rem(part, 4)
            for yy in range(4):
                for hi in range(2):
                    for core in range(2):
                        at = yy * 32 + hi * 16 + core * 8
                        value = turned[at:at + 8]
                        pair = jnp.concatenate([jnp.where(mask, value, 0.0) for mask in masks], axis=0)
                        lhs[lax.rem(c + core, 2), part_z, hi * 2 + part_x, yy * 16:yy * 16 + 16, rows] = pair.astype(bf16)

        lhs_remote(t).start()

    @pl.loop(1, CHUNKS)
    def _(k):
        cot_remote(k).start()

    for e in range(2):
        share(0, e).start()

    z_ring, x_ring, y_ring = (z, z_up, z_dn, z_far), (x, x_up, x_dn, x_far), (y, y_up, y_dn, y_far)
    ring_of = (z_ring, x_ring)
    direct_of = (x_ring, z_ring, y_ring)

    def far_copy(st, k, half):
        far, rfar, send, recv = (rings[st][i] for i in (0, 3, 8, 9))
        rows = far.shape[1] // 2
        return remote(
            far.at[k, pl.ds(half * rows, rows)], rfar.at[k, pl.ds(half * rows, rows)],
            send.at[k, half], recv.at[k, half], ring_of[st][1 + half],
        )

    def near_copy(st, k, way):
        src, dst, send, recv = (rings[st][i] for i in (1 + way, 4 + way, 8, 9))
        return remote(src.at[k], dst.at[k], send.at[k, 2 + way], recv.at[k, 2 + way], ring_of[st][1 + way])

    def emit(st, k, offset, value):
        far, up, dn, _, _, _, own, rel, _, _ = rings[st]
        half = far.shape[1] // 2
        kind = far.dtype
        if offset == 2:
            far[k] = value.astype(kind)
            far_copy(st, k, 0).start()
            far_copy(st, k, 1).start()
        elif offset == 1:
            rel[lax.rem(k, 2), 0] = value[:half]
            up[k, half:] = value[half:].astype(kind)
        elif offset == 3:
            rel[lax.rem(k, 2), 1] = value[half:]
            dn[k, :half] = value[:half].astype(kind)
        else:
            own[lax.rem(k, 4)] = value

    def relay(k):
        for st in range(2):
            _, up, dn, rfar, _, _, _, rel, _, _ = rings[st]
            half = up.shape[1] // 2
            kind = up.dtype
            far_copy(st, k, 0).wait_recv()
            up[k, :half] = (rel[lax.rem(k, 2), 0] + rfar[k, :half].astype(f32)).astype(kind)
            near_copy(st, k, 0).start()
            far_copy(st, k, 1).wait_recv()
            dn[k, half:] = (rel[lax.rem(k, 2), 1] + rfar[k, half:].astype(f32)).astype(kind)
            near_copy(st, k, 1).start()

    def total(st, k):
        near_copy(st, k, 0).wait_recv()
        near_copy(st, k, 1).wait_recv()
        _, _, _, _, rup, rdn, own, _, _, _ = rings[st]
        return own[lax.rem(k, 4)] + rup[k].astype(f32) + rdn[k].astype(f32)

    def direct_copy(st, k, i):
        out, came, _, send, recv = directs[st]
        return remote(out.at[k, i], came.at[k, i], send.at[k, i], recv.at[k, i], direct_of[st][1 + i])

    def spread(st, k, load):
        out, _, own, _, _ = directs[st]
        for i, offset in ((2, 2), (0, 1), (1, 3)):
            out[k, i] = load(lax.rem(direct_of[st][0] + offset, 4)).astype(out.dtype)
            direct_copy(st, k, i).start()
        own[k] = load(direct_of[st][0])

    def collected(st, k):
        _, came, own, _, _ = directs[st]
        for i in range(3):
            direct_copy(st, k, i).wait_recv()
        return own[k] + came[k, 0].astype(f32) + came[k, 1].astype(f32) + came[k, 2].astype(f32)

    def make(k):
        cot_remote(k).wait_recv()
        cols = cot_cols(k)
        for offset in (2, 1, 3, 0):
            at = lax.rem(z + offset, 4)
            value = jnp.dot(lhs[0, at].reshape(256, ROWS), cot_own[:, cols], preferred_element_type=f32)
            value += jnp.dot(lhs_sib[at].reshape(256, ROWS), cot_sib[:, cols], preferred_element_type=f32)
            emit(0, k, offset, value[:, :SPLIT[0]])
            mixed[at] = value[:, SPLIT[0]:].reshape(4, 64, SPLIT[1])
        for offset in (2, 1, 3, 0):
            at = lax.rem(x + offset, 4)
            emit(1, k, offset, mixed[:, at].reshape(256, SPLIT[1]))

    def onward(k):
        for st in range(2):
            tot[st][...] = total(st, k)
            spread(st, k, lambda at: tot[st][pl.ds(pl.multiple_of(at * 64, 64), 64), :])

    def joined(k):
        for st in range(2):
            tot[2][:, st * SPLIT[0]:st * SPLIT[0] + SPLIT[st]] = collected(st, k)
        spread(2, k, lambda at: tot[2][pl.ds(pl.multiple_of(at * 16, 16), 16), :])

    def last(k):
        value = collected(2, k) * grad_factor
        for e in range(2):
            out_buf[:, e, cot_cols(k)] = value[e * 8:e * 8 + 8]

    def grad_copy(turn):
        cols = pl.ds(pl.multiple_of(piece(ORDER[turn]) * 128, 128), 128)
        return pltpu.make_async_copy(grad_buf.at[turn % 2], act_hbm.at[:, :, cols], grad_sem.at[turn])

    def hidden(turn):
        j = ORDER[turn]
        for e in range(2):
            share_wait(j, e)
        if turn >= 2:
            grad_copy(turn - 2).wait()
        q = piece(j)
        cols = pl.ds(pl.multiple_of(q * 128, 128), 128)

        @pl.loop(0, ROWS // 256)
        def _(m):
            rows = pl.ds(pl.multiple_of(m * 256, 256), 256)
            each = lax.dot_general(
                cot_own[rows, :], w_all[q].reshape(256, WIDTH), (((1,), (1,)), ((), ())), preferred_element_type=f32
            )
            for i in range(2):
                part = pl.ds(pl.multiple_of(m * 256 + i * 128, 128), 128)
                row = lax.broadcasted_iota(jnp.int32, (128, 128), 0)
                alive = row < fill_ref[m * 2 + i]
                second = jnp.zeros((128, 128), jnp.int32) + expert_ref[m * 2 + i] == 1
                both = each[i * 128:(i + 1) * 128]
                grad = jnp.where(alive, jnp.where(second, both[:, 128:], both[:, :128]), 0.0)
                gate = pre[0, part, cols].astype(f32)
                up = pre[1, part, cols].astype(f32)
                sig = 1.0 / (1.0 + jnp.exp(-gate))
                grad_buf[turn % 2, part, 0, :] = (grad * up * sig * (1.0 + gate * (1.0 - sig))).astype(bf16)
                grad_buf[turn % 2, part, 1, :] = (grad * (gate * sig)).astype(bf16)

        grad_copy(turn).start()

    @pl.loop(0, CHUNKS)
    def _(k):
        cot_copy(k).wait()

    @pl.loop(0, ROWS // 128)
    def _(t):
        lhs_remote(t).wait_recv()

    @pl.loop(0, CHUNKS + 4)
    def _(t):
        def at(lag, do):
            @pl.when(jnp.logical_and(t >= lag, t < CHUNKS + lag))
            def _():
                do(t - lag)

        def on(when, do):
            @pl.when(t == when)
            def _():
                do()

        for i in range(2):
            on(HOPS[i], lambda: hop(i).start())
        for when, those in EVENTS.items():
            for j, e in those:
                on(when, functools.partial(arrived, j, e))
        at(0, make)
        at(1, relay)
        at(2, onward)
        at(4, joined)

        for when, those in TURNS.items():
            for turn in those:
                on(when, functools.partial(hidden, turn))

    @pl.loop(0, CHUNKS)
    def _(k):
        last(k)

    out = pltpu.make_async_copy(out_buf, wgrad_hbm, out_sem)
    out.start()
    for turn in (6, 7):
        grad_copy(turn).wait()
    out.wait()

    @pl.loop(0, ROWS // 128)
    def _(t):
        lhs_remote(t).wait_send()

    @pl.loop(0, CHUNKS)
    def _(k):
        cot_remote(k).wait_send()
        for st in range(2):
            for i in range(2):
                far_copy(st, k, i).wait_send()
                near_copy(st, k, i).wait_send()
        for st in range(3):
            for i in range(3):
                direct_copy(st, k, i).wait_send()

    for slot in range(len(sends)):
        gather(slot).wait_send()
    for i in range(2):
        hop(i).wait_send()
    for j in range(8):
        for e in range(2):
            share(j, e).wait_send()


def ring_scratch(rows, cols, kind):
    dma = pltpu.SemaphoreType.DMA
    return (
        *[pltpu.VMEM((CHUNKS, rows, cols), kind)] * 6,
        pltpu.VMEM((4, rows, cols), f32),
        pltpu.VMEM((2, 2, rows // 2, cols), f32),
        dma((CHUNKS, 4)),
        dma((CHUNKS, 4)),
    )


def direct_scratch(rows, cols, kind):
    dma = pltpu.SemaphoreType.DMA
    return (
        pltpu.VMEM((CHUNKS, 3, rows, cols), kind),
        pltpu.VMEM((CHUNKS, 3, rows, cols), kind),
        pltpu.VMEM((CHUNKS, rows, cols), f32),
        dma((CHUNKS, 3)),
        dma((CHUNKS, 3)),
    )


def call(cot, pre, w, expert, fill):
    dma = pltpu.SemaphoreType.DMA
    any_space = pl.BlockSpec(memory_space=pl.ANY)
    scalars = pl.BlockSpec(memory_space=pltpu.SMEM)
    return pl.pallas_call(
        kernel,
        out_shape=(
            jax.ShapeDtypeStruct((ROWS, 2, HIDDEN), bf16),
            jax.ShapeDtypeStruct((8, 2, WIDTH), f32),
        ),
        in_specs=[any_space, any_space, any_space, scalars, scalars],
        out_specs=(any_space, any_space),
        scratch_shapes=[
            pltpu.VMEM((ROWS, WIDTH), bf16),
            pltpu.VMEM((ROWS, WIDTH), bf16),
            pltpu.VMEM((2, ROWS, HIDDEN), bf16),
            pltpu.VMEM((2, 4, 4, 64, ROWS), bf16),
            pltpu.VMEM((4, 4, 64, ROWS), bf16),
            pltpu.VMEM((8, 2, 2, 64, WIDTH), bf16),
            pltpu.VMEM((2, ROWS, 2, 128), bf16),
            pltpu.VMEM((8, 2, WIDTH), f32),
            pltpu.VMEM((4, 4, 64, SPLIT[1]), f32),
            tuple(ring_scratch(256, cols, bf16) for cols in SPLIT),
            (
                direct_scratch(64, SPLIT[0], bf16),
                direct_scratch(64, SPLIT[1], bf16),
                direct_scratch(16, WIDE, f32),
            ),
            (pltpu.VMEM((256, SPLIT[0]), f32), pltpu.VMEM((256, SPLIT[1]), f32), pltpu.VMEM((64, WIDE), f32)),
            dma((CHUNKS,)), dma, dma((2,)), dma((8,)), dma,
            dma((CHUNKS,)), dma((CHUNKS,)), dma((6,)), dma((6,)),
            dma((13,)), dma((8, 2)), dma((8, 2)), dma((8, 2)), dma((2,)), dma((2,)),
        ],
        compiler_params=pltpu.CompilerParams(
            collective_id=0, has_side_effects=True, vmem_limit_bytes=60 * 2**20
        ),
        cost_estimate=pl.CostEstimate(flops=24 * 10**9, bytes_accessed=30 * 10**6, transcendentals=0),
    )(cot, pre, w, expert, fill)


def hand_on(act_in, wgrad_in, act_out, wgrad_out, act_buf, wgrad_buf, in_sems, out_sems):
    parts = 8
    rows = ROWS // parts
    slices = [pl.ds(i * rows, rows) for i in range(parts)]
    ins = [pltpu.make_async_copy(act_in.at[r], act_buf.at[r], in_sems.at[i]) for i, r in enumerate(slices)]
    outs = [pltpu.make_async_copy(act_buf.at[r], act_out.at[r], out_sems.at[i]) for i, r in enumerate(slices)]
    ins.append(pltpu.make_async_copy(wgrad_in, wgrad_buf, in_sems.at[parts]))
    outs.append(pltpu.make_async_copy(wgrad_buf, wgrad_out, out_sems.at[parts]))
    for copy in ins:
        copy.start()
    for came, copy in zip(ins, outs):
        came.wait()
        copy.start()
    for copy in outs:
        copy.wait()


def body(cotangent, pre_act, down_weight, tile_expert, tile_fill):
    results = call(
        cotangent, jnp.swapaxes(pre_act, 0, 1), jnp.swapaxes(down_weight, 0, 1), tile_expert, tile_fill
    )
    any_space = pl.BlockSpec(memory_space=pl.ANY)
    return pl.pallas_call(
        hand_on,
        out_shape=tuple(jax.ShapeDtypeStruct(r.shape, r.dtype) for r in results),
        in_specs=[any_space] * 2,
        out_specs=(any_space,) * 2,
        scratch_shapes=[
            pltpu.VMEM((ROWS, 2, HIDDEN), bf16), pltpu.VMEM((8, 2, WIDTH), f32),
            pltpu.SemaphoreType.DMA((9,)), pltpu.SemaphoreType.DMA((9,)),
        ],
        compiler_params=pltpu.CompilerParams(vmem_limit_bytes=16 * 2**20),
    )(*results)


def solution(mesh):
    placed = (
        P(("group", "blk"), None),
        P(("group", "blk"), None, None),
        P("blk", None, None),
        P(("group", "blk")),
        P(("group", "blk")),
    )
    return jax.shard_map(
        body,
        mesh=mesh,
        in_specs=placed,
        out_specs=(P(("group", "blk"), None, None), P(("group", "blk"), None, None)),
        check_vma=False,
    )
```

```python
import functools

import jax
import jax.numpy as jnp
from jax import lax
from jax.experimental import pallas as pl
from jax.experimental.pallas import tpu as pltpu
from jax.sharding import PartitionSpec as P

MESH = pl.DeviceIdType.MESH
grad_factor = 0.015625

ROWS = 768
HIDDEN = 1024
WIDTH = 3584
WIDE = 512
CHUNKS = WIDTH // WIDE
SPLIT = (384, 128)
f32 = jnp.float32
bf16 = jnp.bfloat16

EVENTS = {1: ((1, 0), (2, 1), (4, 0)), 3: ((1, 1), (2, 0)), 4: ((4, 1), (3, 0), (3, 1)),
          6: ((5, 0), (6, 0)), 7: ((5, 1), (6, 1)), 10: ((7, 0), (7, 1))}
HOPS = (1, 2)
ORDER = (0, 1, 2, 4, 3, 5, 6, 7)
TURNS = {2: (0,), 3: (1,), 4: (2,), 5: (3,), 6: (4,), 8: (5,), 9: (6,), 10: (7,)}


def kernel(
    cot_hbm, pre_hbm, w_hbm, expert_ref, fill_ref,
    act_hbm, wgrad_hbm,
    cot_own, cot_sib, raw, pre, lhs, lhs_sib, w_all, grad_buf, out_buf, mixed,
    rings, directs, tot,
    cot_sem, pre_sem, w_sem, grad_sem, out_sem,
    cs_send, cs_recv, ls_send, ls_recv,
    ag_send, ag_recv, sib_send, sib_recv, hop_send, hop_recv,
):
    g = lax.axis_index("group")
    b = lax.axis_index("blk")
    x_lo, z = lax.div(g, 4), lax.rem(g, 4)
    y, c = lax.div(b, 4), lax.rem(b, 2)
    x_hi = lax.rem(lax.div(b, 2), 2)
    x = x_hi * 2 + x_lo

    def device(dx, dy, dz, core):
        xx, yy, zz = lax.rem(x + dx, 4), lax.rem(y + dy, 4), lax.rem(z + dz, 4)
        return (lax.rem(xx, 2) * 4 + zz, yy * 4 + lax.div(xx, 2) * 2 + core)

    other = 1 - c
    sibling = device(0, 0, 0, other)
    x_up, x_dn = device(1, 0, 0, c), device(3, 0, 0, c)
    y_up, y_dn = device(0, 1, 0, c), device(0, 3, 0, c)
    z_up, z_dn = device(0, 0, 1, c), device(0, 0, 3, c)
    x_far, y_far, z_far = device(2, 0, 0, c), device(0, 2, 0, c), device(0, 0, 2, c)
    x_peer = device(3 - 2 * x + 4, 0, 0, c)

    barrier = pltpu.get_barrier_semaphore()
    for peer in (sibling, x_up, x_dn, x_far, y_up, y_dn, y_far, z_up, z_dn, z_far):
        pl.semaphore_signal(barrier, inc=1, device_id=peer, device_id_type=MESH)

    def cot_cols(k):
        return pl.ds(pl.multiple_of(k * WIDE, WIDE), WIDE)

    def cot_copy(k):
        return pltpu.make_async_copy(cot_hbm.at[:, cot_cols(k)], cot_own.at[:, cot_cols(k)], cot_sem.at[k])

    def pre_copy(part):
        cols = pl.ds(pl.multiple_of(part * 128, 128), 128)
        return pltpu.make_async_copy(pre_hbm.at[:, :, cols], raw.at[part], pre_sem.at[part])

    q_own = y * 2 + x_hi

    def w_copy(e):
        return pltpu.make_async_copy(w_hbm.at[e], w_all.at[q_own, e, c], w_sem.at[e])

    for e in range(2):
        w_copy(e).start()

    @pl.loop(0, 8)
    def _(part):
        pre_copy(part).start()

    @pl.loop(0, CHUNKS)
    def _(k):
        cot_copy(k).start()

    pl.semaphore_wait(barrier, 10)

    def remote(src, dst, send, recv, device_id):
        return pltpu.make_async_remote_copy(
            src_ref=src, dst_ref=dst, send_sem=send, recv_sem=recv, device_id=device_id, device_id_type=MESH
        )

    def lhs_remote(t):
        rows = pl.ds(pl.multiple_of(t * 128, 128), 128)
        return remote(
            lhs.at[1, :, :, :, rows], lhs_sib.at[:, :, :, rows], ls_send.at[t], ls_recv.at[t], sibling
        )

    def cot_remote(k):
        return remote(
            cot_hbm.at[:, cot_cols(k)], cot_sib.at[:, cot_cols(k)], cs_send.at[k], cs_recv.at[k], sibling
        )

    def piece(j):
        yy = lax.rem(y + (0, 3, 1, 2)[j % 4], 4)
        return yy * 2 + (x_hi if j < 4 else 1 - x_hi)

    def gather(slot):
        src_j, dst_j, e, device_id = sends[slot]
        block = w_all.at[piece(src_j), e, c]
        return remote(block, block, ag_send.at[slot], ag_recv.at[dst_j, e], device_id)

    def hop(i):
        block = w_all.at[piece(0), 1, c, pl.ds(i * 32, 32)]
        return remote(block, block, hop_send.at[i], hop_recv.at[i], x_peer)

    def hop_wait(i):
        block = w_all.at[piece(4), 1, c, pl.ds(i * 32, 32)]
        remote(block, block, hop_send.at[i], hop_recv.at[i], x_peer).wait_recv()

    def gather_wait(j, e):
        if (j, e) == (4, 1):
            for i in range(2):
                hop_wait(i)
        else:
            block = w_all.at[piece(j), e, c]
            remote(block, block, ag_send.at[0], ag_recv.at[j, e], sibling).wait_recv()

    def share(j, e):
        block = w_all.at[piece(j), e, c]
        return remote(block, block, sib_send.at[j, e], sib_recv.at[j, e], sibling)

    def share_wait(j, e):
        block = w_all.at[piece(j), e, other]
        remote(block, block, sib_send.at[j, e], sib_recv.at[j, e], sibling).wait_recv()

    sends = [(0, 1, 0, y_up), (0, 2, 1, y_dn), (0, 4, 0, x_peer), (0, 1, 1, y_up), (0, 2, 0, y_dn)]
    sends += [(1, 3, 0, y_up), (2, 3, 1, y_dn)]
    for e in range(2):
        sends += [(4, 5, e, y_up), (4, 6, e, y_dn)]
    sends += [(5, 7, 0, y_up), (6, 7, 1, y_dn)]

    def gather_start(j, e):
        for slot, (src_j, _, src_e, _) in enumerate(sends):
            if (src_j, src_e) == (j, e):
                gather(slot).start()

    def arrived(j, e):
        gather_wait(j, e)
        gather_start(j, e)
        share(j, e).start()

    cot_remote(0).start()
    for e in range(2):
        w_copy(e).wait()
    for slot in range(5):
        gather(slot).start()

    for part in range(8):
        pre_copy(part).wait()

        @pl.loop(0, ROWS // 128)
        def _(t):
            rows = pl.ds(pl.multiple_of(t * 128, 128), 128)
            both = raw[part, rows].astype(f32)
            for i in range(2):
                pre[i, rows, part * 128:part * 128 + 128] = both[:, i, :].astype(bf16)

    @pl.loop(0, ROWS // 128)
    def _(t):
        rows = pl.ds(pl.multiple_of(t * 128, 128), 128)
        lane = lax.broadcasted_iota(jnp.int32, (8, 128), 1)
        alive = lane < fill_ref[t]
        chosen = jnp.zeros((8, 128), jnp.int32) + expert_ref[t]
        masks = [jnp.logical_and(alive, chosen == e) for e in range(2)]

        @pl.loop(0, 8)
        def _(part):
            cols = pl.ds(pl.multiple_of(part * 128, 128), 128)
            gate = pre[0, rows, cols].astype(f32)
            up = pre[1, rows, cols].astype(f32)
            sig = jax.nn.sigmoid(gate)
            turned = jnp.transpose(gate * sig * up)
            part_x, part_z = lax.div(part, 4), lax.rem(part, 4)
            for yy in range(4):
                for hi in range(2):
                    for core in range(2):
                        at = yy * 32 + hi * 16 + core * 8
                        value = turned[at:at + 8]
                        pair = jnp.concatenate([jnp.where(mask, value, 0.0) for mask in masks], axis=0)
                        lhs[lax.rem(c + core, 2), part_z, hi * 2 + part_x, yy * 16:yy * 16 + 16, rows] = pair.astype(bf16)

        lhs_remote(t).start()

    @pl.loop(1, CHUNKS)
    def _(k):
        cot_remote(k).start()

    for e in range(2):
        share(0, e).start()

    z_ring, x_ring, y_ring = (z, z_up, z_dn, z_far), (x, x_up, x_dn, x_far), (y, y_up, y_dn, y_far)
    ring_of = (z_ring, x_ring)
    direct_of = (x_ring, z_ring, y_ring)

    def far_copy(st, k, half):
        far, rfar, send, recv = (rings[st][i] for i in (0, 3, 8, 9))
        rows = far.shape[1] // 2
        return remote(
            far.at[k, pl.ds(half * rows, rows)], rfar.at[k, pl.ds(half * rows, rows)],
            send.at[k, half], recv.at[k, half], ring_of[st][1 + half],
        )

    def near_copy(st, k, way):
        src, dst, send, recv = (rings[st][i] for i in (1 + way, 4 + way, 8, 9))
        return remote(src.at[k], dst.at[k], send.at[k, 2 + way], recv.at[k, 2 + way], ring_of[st][1 + way])

    def emit(st, k, offset, value):
        far, up, dn, _, _, _, own, rel, _, _ = rings[st]
        half = far.shape[1] // 2
        kind = far.dtype
        if offset == 2:
            far[k] = value.astype(kind)
            far_copy(st, k, 0).start()
            far_copy(st, k, 1).start()
        elif offset == 1:
            rel[lax.rem(k, 2), 0] = value[:half]
            up[k, half:] = value[half:].astype(kind)
        elif offset == 3:
            rel[lax.rem(k, 2), 1] = value[half:]
            dn[k, :half] = value[:half].astype(kind)
        else:
            own[lax.rem(k, 4)] = value

    def relay(k):
        for st in range(2):
            _, up, dn, rfar, _, _, _, rel, _, _ = rings[st]
            half = up.shape[1] // 2
            kind = up.dtype
            far_copy(st, k, 0).wait_recv()
            up[k, :half] = (rel[lax.rem(k, 2), 0] + rfar[k, :half].astype(f32)).astype(kind)
            near_copy(st, k, 0).start()
            far_copy(st, k, 1).wait_recv()
            dn[k, half:] = (rel[lax.rem(k, 2), 1] + rfar[k, half:].astype(f32)).astype(kind)
            near_copy(st, k, 1).start()

    def total(st, k):
        near_copy(st, k, 0).wait_recv()
        near_copy(st, k, 1).wait_recv()
        _, _, _, _, rup, rdn, own, _, _, _ = rings[st]
        return own[lax.rem(k, 4)] + rup[k].astype(f32) + rdn[k].astype(f32)

    def direct_copy(st, k, i):
        out, came, _, send, recv = directs[st]
        return remote(out.at[k, i], came.at[k, i], send.at[k, i], recv.at[k, i], direct_of[st][1 + i])

    def spread(st, k, load):
        out, _, own, _, _ = directs[st]
        for i, offset in ((2, 2), (0, 1), (1, 3)):
            out[k, i] = load(lax.rem(direct_of[st][0] + offset, 4)).astype(out.dtype)
            direct_copy(st, k, i).start()
        own[k] = load(direct_of[st][0])

    def collected(st, k):
        _, came, own, _, _ = directs[st]
        for i in range(3):
            direct_copy(st, k, i).wait_recv()
        return own[k] + came[k, 0].astype(f32) + came[k, 1].astype(f32) + came[k, 2].astype(f32)

    def make(k):
        cot_remote(k).wait_recv()
        cols = cot_cols(k)
        for offset in (2, 1, 3, 0):
            at = lax.rem(z + offset, 4)
            value = jnp.dot(lhs[0, at].reshape(256, ROWS), cot_own[:, cols], preferred_element_type=f32)
            value += jnp.dot(lhs_sib[at].reshape(256, ROWS), cot_sib[:, cols], preferred_element_type=f32)
            emit(0, k, offset, value[:, :SPLIT[0]])
            mixed[at] = value[:, SPLIT[0]:].reshape(4, 64, SPLIT[1])
        for offset in (2, 1, 3, 0):
            at = lax.rem(x + offset, 4)
            emit(1, k, offset, mixed[:, at].reshape(256, SPLIT[1]))

    def onward(k):
        for st in range(2):
            tot[st][...] = total(st, k)
            spread(st, k, lambda at: tot[st][pl.ds(pl.multiple_of(at * 64, 64), 64), :])

    def joined(k):
        for st in range(2):
            tot[2][:, st * SPLIT[0]:st * SPLIT[0] + SPLIT[st]] = collected(st, k)
        spread(2, k, lambda at: tot[2][pl.ds(pl.multiple_of(at * 16, 16), 16), :])

    def last(k):
        value = collected(2, k) * grad_factor
        for e in range(2):
            out_buf[:, e, cot_cols(k)] = value[e * 8:e * 8 + 8]

    def grad_copy(turn):
        cols = pl.ds(pl.multiple_of(piece(ORDER[turn]) * 128, 128), 128)
        return pltpu.make_async_copy(grad_buf.at[turn % 2], act_hbm.at[:, :, cols], grad_sem.at[turn])

    def hidden(turn):
        j = ORDER[turn]
        for e in range(2):
            share_wait(j, e)
        if turn >= 2:
            grad_copy(turn - 2).wait()
        q = piece(j)
        cols = pl.ds(pl.multiple_of(q * 128, 128), 128)

        @pl.loop(0, ROWS // 256)
        def _(m):
            rows = pl.ds(pl.multiple_of(m * 256, 256), 256)
            each = lax.dot_general(
                cot_own[rows, :], w_all[q].reshape(256, WIDTH), (((1,), (1,)), ((), ())), preferred_element_type=f32
            )
            for i in range(2):
                part = pl.ds(pl.multiple_of(m * 256 + i * 128, 128), 128)
                row = lax.broadcasted_iota(jnp.int32, (128, 128), 0)
                alive = row < fill_ref[m * 2 + i]
                second = jnp.zeros((128, 128), jnp.int32) + expert_ref[m * 2 + i] == 1
                both = each[i * 128:(i + 1) * 128]
                grad = jnp.where(alive, jnp.where(second, both[:, 128:], both[:, :128]), 0.0)
                gate = pre[0, part, cols].astype(f32)
                up = pre[1, part, cols].astype(f32)
                sig = jax.nn.sigmoid(gate)
                grad_buf[turn % 2, part, 0, :] = (grad * up * sig * (1.0 + gate * (1.0 - sig))).astype(bf16)
                grad_buf[turn % 2, part, 1, :] = (grad * (gate * sig)).astype(bf16)

        grad_copy(turn).start()

    @pl.loop(0, CHUNKS)
    def _(k):
        cot_copy(k).wait()

    @pl.loop(0, ROWS // 128)
    def _(t):
        lhs_remote(t).wait_recv()

    @pl.loop(0, CHUNKS + 4)
    def _(t):
        def at(lag, do):
            @pl.when(jnp.logical_and(t >= lag, t < CHUNKS + lag))
            def _():
                do(t - lag)

        def on(when, do):
            @pl.when(t == when)
            def _():
                do()

        for i in range(2):
            on(HOPS[i], lambda: hop(i).start())
        for when, those in EVENTS.items():
            for j, e in those:
                on(when, functools.partial(arrived, j, e))
        at(0, make)
        at(1, relay)
        at(2, onward)
        at(4, joined)

        for when, those in TURNS.items():
            for turn in those:
                on(when, functools.partial(hidden, turn))

    @pl.loop(0, CHUNKS)
    def _(k):
        last(k)

    out = pltpu.make_async_copy(out_buf, wgrad_hbm, out_sem)
    out.start()
    for turn in (6, 7):
        grad_copy(turn).wait()
    out.wait()

    @pl.loop(0, ROWS // 128)
    def _(t):
        lhs_remote(t).wait_send()

    @pl.loop(0, CHUNKS)
    def _(k):
        cot_remote(k).wait_send()
        for st in range(2):
            for i in range(2):
                far_copy(st, k, i).wait_send()
                near_copy(st, k, i).wait_send()
        for st in range(3):
            for i in range(3):
                direct_copy(st, k, i).wait_send()

    for slot in range(len(sends)):
        gather(slot).wait_send()
    for i in range(2):
        hop(i).wait_send()
    for j in range(8):
        for e in range(2):
            share(j, e).wait_send()


def ring_scratch(rows, cols, kind):
    dma = pltpu.SemaphoreType.DMA
    return (
        *[pltpu.VMEM((CHUNKS, rows, cols), kind)] * 6,
        pltpu.VMEM((4, rows, cols), f32),
        pltpu.VMEM((2, 2, rows // 2, cols), f32),
        dma((CHUNKS, 4)),
        dma((CHUNKS, 4)),
    )


def direct_scratch(rows, cols, kind):
    dma = pltpu.SemaphoreType.DMA
    return (
        pltpu.VMEM((CHUNKS, 3, rows, cols), kind),
        pltpu.VMEM((CHUNKS, 3, rows, cols), kind),
        pltpu.VMEM((CHUNKS, rows, cols), f32),
        dma((CHUNKS, 3)),
        dma((CHUNKS, 3)),
    )


def call(cot, pre, w, expert, fill):
    dma = pltpu.SemaphoreType.DMA
    any_space = pl.BlockSpec(memory_space=pl.ANY)
    scalars = pl.BlockSpec(memory_space=pltpu.SMEM)
    return pl.pallas_call(
        kernel,
        out_shape=(
            jax.ShapeDtypeStruct((ROWS, 2, HIDDEN), bf16),
            jax.ShapeDtypeStruct((8, 2, WIDTH), f32),
        ),
        in_specs=[any_space, pl.BlockSpec(memory_space=pltpu.HBM), any_space, scalars, scalars],
        out_specs=(any_space, any_space),
        scratch_shapes=[
            pltpu.VMEM((ROWS, WIDTH), bf16),
            pltpu.VMEM((ROWS, WIDTH), bf16),
            pltpu.VMEM((8, ROWS, 2, 128), bf16),
            pltpu.VMEM((2, ROWS, HIDDEN), bf16),
            pltpu.VMEM((2, 4, 4, 64, ROWS), bf16),
            pltpu.VMEM((4, 4, 64, ROWS), bf16),
            pltpu.VMEM((8, 2, 2, 64, WIDTH), bf16),
            pltpu.VMEM((2, ROWS, 2, 128), bf16),
            pltpu.VMEM((8, 2, WIDTH), f32),
            pltpu.VMEM((4, 4, 64, SPLIT[1]), f32),
            tuple(ring_scratch(256, cols, bf16) for cols in SPLIT),
            (
                direct_scratch(64, SPLIT[0], bf16),
                direct_scratch(64, SPLIT[1], bf16),
                direct_scratch(16, WIDE, f32),
            ),
            (pltpu.VMEM((256, SPLIT[0]), f32), pltpu.VMEM((256, SPLIT[1]), f32), pltpu.VMEM((64, WIDE), f32)),
            dma((CHUNKS,)), dma((8,)), dma((2,)), dma((8,)), dma,
            dma((CHUNKS,)), dma((CHUNKS,)), dma((6,)), dma((6,)),
            dma((13,)), dma((8, 2)), dma((8, 2)), dma((8, 2)), dma((2,)), dma((2,)),
        ],
        compiler_params=pltpu.CompilerParams(
            collective_id=0, has_side_effects=True, vmem_limit_bytes=60 * 2**20
        ),
        cost_estimate=pl.CostEstimate(flops=24 * 10**9, bytes_accessed=30 * 10**6, transcendentals=0),
    )(cot, pre, w, expert, fill)


def hand_on(act_in, wgrad_in, act_out, wgrad_out, act_buf, wgrad_buf, in_sems, out_sems):
    parts = 4
    rows = ROWS // parts
    slices = [pl.ds(i * rows, rows) for i in range(parts)]
    ins = [pltpu.make_async_copy(act_in.at[r], act_buf.at[r], in_sems.at[i]) for i, r in enumerate(slices)]
    outs = [pltpu.make_async_copy(act_buf.at[r], act_out.at[r], out_sems.at[i]) for i, r in enumerate(slices)]
    ins.append(pltpu.make_async_copy(wgrad_in, wgrad_buf, in_sems.at[parts]))
    outs.append(pltpu.make_async_copy(wgrad_buf, wgrad_out, out_sems.at[parts]))
    for copy in ins:
        copy.start()
    for came, copy in zip(ins, outs):
        came.wait()
        copy.start()
    for copy in outs:
        copy.wait()


def body(cotangent, pre_act, down_weight, tile_expert, tile_fill):
    results = call(
        cotangent, pre_act, jnp.swapaxes(down_weight, 0, 1), tile_expert, tile_fill
    )
    any_space = pl.BlockSpec(memory_space=pl.ANY)
    return pl.pallas_call(
        hand_on,
        out_shape=tuple(jax.ShapeDtypeStruct(r.shape, r.dtype) for r in results),
        in_specs=[pl.BlockSpec(memory_space=pltpu.HBM)] * 2,
        out_specs=(any_space,) * 2,
        scratch_shapes=[
            pltpu.VMEM((ROWS, 2, HIDDEN), bf16), pltpu.VMEM((8, 2, WIDTH), f32),
            pltpu.SemaphoreType.DMA((9,)), pltpu.SemaphoreType.DMA((9,)),
        ],
        compiler_params=pltpu.CompilerParams(vmem_limit_bytes=60 * 2**20),
    )(*results)


def solution(mesh):
    placed = (
        P(("group", "blk"), None),
        P(("group", "blk"), None, None),
        P("blk", None, None),
        P(("group", "blk")),
        P(("group", "blk")),
    )
    return jax.shard_map(
        body,
        mesh=mesh,
        in_specs=placed,
        out_specs=(P(("group", "blk"), None, None), P(("group", "blk"), None, None)),
        check_vma=False,
    )
```

```python
import functools

import jax
import jax.numpy as jnp
from jax import lax
from jax.experimental import pallas as pl
from jax.experimental.pallas import tpu as pltpu
from jax.sharding import PartitionSpec as P

MESH = pl.DeviceIdType.MESH
grad_factor = 0.015625

ROWS = 768
HIDDEN = 1024
WIDTH = 3584
WIDE = 512
CHUNKS = WIDTH // WIDE
SPLIT = (256, 256)
f32 = jnp.float32
bf16 = jnp.bfloat16

EVENTS = {0: ((1, 0), (2, 1)), 1: ((4, 0),), 2: ((1, 1),), 3: ((2, 0),), 4: ((3, 0), (4, 1)), 5: ((5, 0),),
          6: ((3, 1), (6, 1)), 7: ((5, 1),), 8: ((6, 0),), 9: ((7, 0), (7, 1))}
HOPS = (0, 3)
ORDER = (0, 1, 2, 4, 3, 5, 6, 7)
TURNS = {2: (0,), 3: (1, 2), 5: (3,), 6: (4,), 7: (5,), 9: (6,), 10: (7,)}


def kernel(
    cot_hbm, pre_hbm, w_hbm, expert_ref, fill_ref,
    act_hbm, wgrad_hbm,
    cot_own, cot_sib, raw, pre, lhs, lhs_sib, w_all, grad_buf, out_buf, mixed,
    rings, directs, tot,
    cot_sem, pre_sem, w_sem, grad_sem, out_sem,
    cs_send, cs_recv, ls_send, ls_recv,
    ag_send, ag_recv, sib_send, sib_recv, hop_send, hop_recv,
):
    g = lax.axis_index("group")
    b = lax.axis_index("blk")
    x_lo, z = lax.div(g, 4), lax.rem(g, 4)
    y, c = lax.div(b, 4), lax.rem(b, 2)
    x_hi = lax.rem(lax.div(b, 2), 2)
    x = x_hi * 2 + x_lo

    def device(dx, dy, dz, core):
        xx, yy, zz = lax.rem(x + dx, 4), lax.rem(y + dy, 4), lax.rem(z + dz, 4)
        return (lax.rem(xx, 2) * 4 + zz, yy * 4 + lax.div(xx, 2) * 2 + core)

    other = 1 - c
    sibling = device(0, 0, 0, other)
    x_up, x_dn = device(1, 0, 0, c), device(3, 0, 0, c)
    y_up, y_dn = device(0, 1, 0, c), device(0, 3, 0, c)
    z_up, z_dn = device(0, 0, 1, c), device(0, 0, 3, c)
    x_far, y_far, z_far = device(2, 0, 0, c), device(0, 2, 0, c), device(0, 0, 2, c)
    x_peer = device(3 - 2 * x + 4, 0, 0, c)

    barrier = pltpu.get_barrier_semaphore()
    for peer in (sibling, x_up, x_dn, x_far, y_up, y_dn, y_far, z_up, z_dn, z_far):
        pl.semaphore_signal(barrier, inc=1, device_id=peer, device_id_type=MESH)

    def cot_cols(k):
        return pl.ds(pl.multiple_of(k * WIDE, WIDE), WIDE)

    def cot_copy(k):
        return pltpu.make_async_copy(cot_hbm.at[:, cot_cols(k)], cot_own.at[:, cot_cols(k)], cot_sem.at[k])

    def pre_copy(part):
        cols = pl.ds(pl.multiple_of(part * 128, 128), 128)
        return pltpu.make_async_copy(pre_hbm.at[:, :, cols], raw.at[part], pre_sem.at[part])

    q_own = y * 2 + x_hi

    def w_copy(e):
        return pltpu.make_async_copy(w_hbm.at[e], w_all.at[q_own, e, c], w_sem.at[e])

    for e in range(2):
        w_copy(e).start()

    @pl.loop(0, 8)
    def _(part):
        pre_copy(part).start()

    @pl.loop(0, CHUNKS)
    def _(k):
        cot_copy(k).start()

    pl.semaphore_wait(barrier, 10)

    def remote(src, dst, send, recv, device_id):
        return pltpu.make_async_remote_copy(
            src_ref=src, dst_ref=dst, send_sem=send, recv_sem=recv, device_id=device_id, device_id_type=MESH
        )

    def lhs_remote(t):
        rows = pl.ds(pl.multiple_of(t * 128, 128), 128)
        return remote(
            lhs.at[1, :, :, :, rows], lhs_sib.at[:, :, :, rows], ls_send.at[t], ls_recv.at[t], sibling
        )

    def cot_remote(k):
        return remote(
            cot_hbm.at[:, cot_cols(k)], cot_sib.at[:, cot_cols(k)], cs_send.at[k], cs_recv.at[k], sibling
        )

    def piece(j):
        yy = lax.rem(y + (0, 3, 1, 2)[j % 4], 4)
        return yy * 2 + (x_hi if j < 4 else 1 - x_hi)

    def gather(slot):
        src_j, dst_j, e, device_id = sends[slot]
        block = w_all.at[piece(src_j), e, c]
        return remote(block, block, ag_send.at[slot], ag_recv.at[dst_j, e], device_id)

    def hop(i):
        block = w_all.at[piece(0), 1, c, pl.ds(i * 32, 32)]
        return remote(block, block, hop_send.at[i], hop_recv.at[i], x_peer)

    def hop_wait(i):
        block = w_all.at[piece(4), 1, c, pl.ds(i * 32, 32)]
        remote(block, block, hop_send.at[i], hop_recv.at[i], x_peer).wait_recv()

    def gather_wait(j, e):
        if (j, e) == (4, 1):
            for i in range(2):
                hop_wait(i)
        else:
            block = w_all.at[piece(j), e, c]
            remote(block, block, ag_send.at[0], ag_recv.at[j, e], sibling).wait_recv()

    def share(j, e):
        block = w_all.at[piece(j), e, c]
        return remote(block, block, sib_send.at[j, e], sib_recv.at[j, e], sibling)

    def share_wait(j, e):
        block = w_all.at[piece(j), e, other]
        remote(block, block, sib_send.at[j, e], sib_recv.at[j, e], sibling).wait_recv()

    sends = [(0, 1, 0, y_up), (0, 2, 1, y_dn), (0, 4, 0, x_peer), (0, 1, 1, y_up), (0, 2, 0, y_dn)]
    sends += [(1, 3, 0, y_up), (2, 3, 1, y_dn)]
    for e in range(2):
        sends += [(4, 5, e, y_up), (4, 6, e, y_dn)]
    sends += [(5, 7, 0, y_up), (6, 7, 1, y_dn)]

    def gather_start(j, e):
        for slot, (src_j, _, src_e, _) in enumerate(sends):
            if (src_j, src_e) == (j, e):
                gather(slot).start()

    def arrived(j, e):
        gather_wait(j, e)
        gather_start(j, e)
        share(j, e).start()

    cot_remote(0).start()
    for e in range(2):
        w_copy(e).wait()
    for slot in range(5):
        gather(slot).start()

    for part in range(8):
        pre_copy(part).wait()

        @pl.loop(0, ROWS // 128)
        def _(t):
            rows = pl.ds(pl.multiple_of(t * 128, 128), 128)
            both = raw[part, rows].astype(f32)
            for i in range(2):
                pre[i, rows, part * 128:part * 128 + 128] = both[:, i, :].astype(bf16)

    @pl.loop(0, ROWS // 128)
    def _(t):
        rows = pl.ds(pl.multiple_of(t * 128, 128), 128)
        lane = lax.broadcasted_iota(jnp.int32, (8, 128), 1)
        alive = lane < fill_ref[t]
        chosen = jnp.zeros((8, 128), jnp.int32) + expert_ref[t]
        masks = [jnp.logical_and(alive, chosen == e) for e in range(2)]

        @pl.loop(0, 8)
        def _(part):
            cols = pl.ds(pl.multiple_of(part * 128, 128), 128)
            gate = pre[0, rows, cols].astype(f32)
            up = pre[1, rows, cols].astype(f32)
            sig = jax.nn.sigmoid(gate)
            turned = jnp.transpose(gate * sig * up)
            part_x, part_z = lax.div(part, 4), lax.rem(part, 4)
            for yy in range(4):
                for hi in range(2):
                    for core in range(2):
                        at = yy * 32 + hi * 16 + core * 8
                        value = turned[at:at + 8]
                        pair = jnp.concatenate([jnp.where(mask, value, 0.0) for mask in masks], axis=0)
                        lhs[lax.rem(c + core, 2), part_z, hi * 2 + part_x, yy * 16:yy * 16 + 16, rows] = pair.astype(bf16)

        lhs_remote(t).start()

    @pl.loop(1, CHUNKS)
    def _(k):
        cot_remote(k).start()

    for e in range(2):
        share(0, e).start()

    z_ring, x_ring, y_ring = (z, z_up, z_dn, z_far), (x, x_up, x_dn, x_far), (y, y_up, y_dn, y_far)
    ring_of = (z_ring, x_ring)
    direct_of = (x_ring, z_ring, y_ring)

    def far_copy(st, k, half):
        far, rfar, send, recv = (rings[st][i] for i in (0, 3, 8, 9))
        rows = far.shape[1] // 2
        return remote(
            far.at[k, pl.ds(half * rows, rows)], rfar.at[k, pl.ds(half * rows, rows)],
            send.at[k, half], recv.at[k, half], ring_of[st][1 + half],
        )

    def near_copy(st, k, way):
        src, dst, send, recv = (rings[st][i] for i in (1 + way, 4 + way, 8, 9))
        return remote(src.at[k], dst.at[k], send.at[k, 2 + way], recv.at[k, 2 + way], ring_of[st][1 + way])

    def emit(st, k, offset, value):
        far, up, dn, _, _, _, own, rel, _, _ = rings[st]
        half = far.shape[1] // 2
        kind = far.dtype
        if offset == 2:
            far[k] = value.astype(kind)
            far_copy(st, k, 0).start()
            far_copy(st, k, 1).start()
        elif offset == 1:
            rel[lax.rem(k, 2), 0] = value[:half]
            up[k, half:] = value[half:].astype(kind)
        elif offset == 3:
            rel[lax.rem(k, 2), 1] = value[half:]
            dn[k, :half] = value[:half].astype(kind)
        else:
            own[lax.rem(k, 4)] = value

    def relay(k):
        for st in range(2):
            _, up, dn, rfar, _, _, _, rel, _, _ = rings[st]
            half = up.shape[1] // 2
            kind = up.dtype
            far_copy(st, k, 0).wait_recv()
            up[k, :half] = (rel[lax.rem(k, 2), 0] + rfar[k, :half].astype(f32)).astype(kind)
            near_copy(st, k, 0).start()
            far_copy(st, k, 1).wait_recv()
            dn[k, half:] = (rel[lax.rem(k, 2), 1] + rfar[k, half:].astype(f32)).astype(kind)
            near_copy(st, k, 1).start()

    def total(st, k):
        near_copy(st, k, 0).wait_recv()
        near_copy(st, k, 1).wait_recv()
        _, _, _, _, rup, rdn, own, _, _, _ = rings[st]
        return own[lax.rem(k, 4)] + rup[k].astype(f32) + rdn[k].astype(f32)

    def direct_copy(st, k, i):
        out, came, _, send, recv = directs[st]
        return remote(out.at[k, i], came.at[k, i], send.at[k, i], recv.at[k, i], direct_of[st][1 + i])

    def spread(st, k, load):
        out, _, own, _, _ = directs[st]
        for i, offset in ((2, 2), (0, 1), (1, 3)):
            out[k, i] = load(lax.rem(direct_of[st][0] + offset, 4)).astype(out.dtype)
            direct_copy(st, k, i).start()
        own[k] = load(direct_of[st][0])

    def collected(st, k):
        _, came, own, _, _ = directs[st]
        for i in range(3):
            direct_copy(st, k, i).wait_recv()
        return own[k] + came[k, 0].astype(f32) + came[k, 1].astype(f32) + came[k, 2].astype(f32)

    def make(k):
        cot_remote(k).wait_recv()
        cols = cot_cols(k)
        for offset in (2, 1, 3, 0):
            at = lax.rem(z + offset, 4)
            value = jnp.dot(lhs[0, at].reshape(256, ROWS), cot_own[:, cols], preferred_element_type=f32)
            value += jnp.dot(lhs_sib[at].reshape(256, ROWS), cot_sib[:, cols], preferred_element_type=f32)
            emit(0, k, offset, value[:, :SPLIT[0]])
            mixed[at] = value[:, SPLIT[0]:].reshape(4, 64, SPLIT[1])
        for offset in (2, 1, 3, 0):
            at = lax.rem(x + offset, 4)
            emit(1, k, offset, mixed[:, at].reshape(256, SPLIT[1]))

    def onward(k):
        for st in range(2):
            tot[st][...] = total(st, k)
            spread(st, k, lambda at: tot[st][pl.ds(pl.multiple_of(at * 64, 64), 64), :])

    def joined(k):
        for st in range(2):
            tot[2][:, st * SPLIT[0]:st * SPLIT[0] + SPLIT[st]] = collected(st, k)
        spread(2, k, lambda at: tot[2][pl.ds(pl.multiple_of(at * 16, 16), 16), :])

    def last(k):
        value = collected(2, k) * grad_factor
        for e in range(2):
            out_buf[:, e, cot_cols(k)] = value[e * 8:e * 8 + 8]

    def grad_copy(turn):
        cols = pl.ds(pl.multiple_of(piece(ORDER[turn]) * 128, 128), 128)
        return pltpu.make_async_copy(grad_buf.at[turn % 2], act_hbm.at[:, :, cols], grad_sem.at[turn])

    def hidden(turn):
        j = ORDER[turn]
        for e in range(2):
            share_wait(j, e)
        if turn >= 2:
            grad_copy(turn - 2).wait()
        q = piece(j)
        cols = pl.ds(pl.multiple_of(q * 128, 128), 128)

        @pl.loop(0, ROWS // 256)
        def _(m):
            rows = pl.ds(pl.multiple_of(m * 256, 256), 256)
            each = lax.dot_general(
                cot_own[rows, :], w_all[q].reshape(256, WIDTH), (((1,), (1,)), ((), ())), preferred_element_type=f32
            )
            for i in range(2):
                part = pl.ds(pl.multiple_of(m * 256 + i * 128, 128), 128)
                row = lax.broadcasted_iota(jnp.int32, (128, 128), 0)
                alive = row < fill_ref[m * 2 + i]
                second = jnp.zeros((128, 128), jnp.int32) + expert_ref[m * 2 + i] == 1
                both = each[i * 128:(i + 1) * 128]
                grad = jnp.where(alive, jnp.where(second, both[:, 128:], both[:, :128]), 0.0)
                gate = pre[0, part, cols].astype(f32)
                up = pre[1, part, cols].astype(f32)
                sig = jax.nn.sigmoid(gate)
                grad_buf[turn % 2, part, 0, :] = (grad * up * sig * (1.0 + gate * (1.0 - sig))).astype(bf16)
                grad_buf[turn % 2, part, 1, :] = (grad * (gate * sig)).astype(bf16)

        grad_copy(turn).start()

    @pl.loop(0, CHUNKS)
    def _(k):
        cot_copy(k).wait()

    @pl.loop(0, ROWS // 128)
    def _(t):
        lhs_remote(t).wait_recv()

    @pl.loop(0, CHUNKS + 4)
    def _(t):
        def at(lag, do):
            @pl.when(jnp.logical_and(t >= lag, t < CHUNKS + lag))
            def _():
                do(t - lag)

        def on(when, do):
            @pl.when(t == when)
            def _():
                do()

        for i in range(2):
            on(HOPS[i], lambda: hop(i).start())
        for when, those in EVENTS.items():
            for j, e in those:
                on(when, functools.partial(arrived, j, e))
        at(0, make)
        at(1, relay)
        at(2, onward)
        at(4, joined)

        for when, those in TURNS.items():
            for turn in those:
                on(when, functools.partial(hidden, turn))

    @pl.loop(0, CHUNKS)
    def _(k):
        last(k)

    out = pltpu.make_async_copy(out_buf, wgrad_hbm, out_sem)
    out.start()
    for turn in (6, 7):
        grad_copy(turn).wait()
    out.wait()

    @pl.loop(0, ROWS // 128)
    def _(t):
        lhs_remote(t).wait_send()

    @pl.loop(0, CHUNKS)
    def _(k):
        cot_remote(k).wait_send()
        for st in range(2):
            for i in range(2):
                far_copy(st, k, i).wait_send()
                near_copy(st, k, i).wait_send()
        for st in range(3):
            for i in range(3):
                direct_copy(st, k, i).wait_send()

    for slot in range(len(sends)):
        gather(slot).wait_send()
    for i in range(2):
        hop(i).wait_send()
    for j in range(8):
        for e in range(2):
            share(j, e).wait_send()


def ring_scratch(rows, cols, kind):
    dma = pltpu.SemaphoreType.DMA
    return (
        *[pltpu.VMEM((CHUNKS, rows, cols), kind)] * 6,
        pltpu.VMEM((4, rows, cols), f32),
        pltpu.VMEM((2, 2, rows // 2, cols), f32),
        dma((CHUNKS, 4)),
        dma((CHUNKS, 4)),
    )


def direct_scratch(rows, cols, kind):
    dma = pltpu.SemaphoreType.DMA
    return (
        pltpu.VMEM((CHUNKS, 3, rows, cols), kind),
        pltpu.VMEM((CHUNKS, 3, rows, cols), kind),
        pltpu.VMEM((CHUNKS, rows, cols), f32),
        dma((CHUNKS, 3)),
        dma((CHUNKS, 3)),
    )


def call(cot, pre, w, expert, fill):
    dma = pltpu.SemaphoreType.DMA
    any_space = pl.BlockSpec(memory_space=pl.ANY)
    scalars = pl.BlockSpec(memory_space=pltpu.SMEM)
    return pl.pallas_call(
        kernel,
        out_shape=(
            jax.ShapeDtypeStruct((ROWS, 2, HIDDEN), bf16),
            jax.ShapeDtypeStruct((8, 2, WIDTH), f32),
        ),
        in_specs=[any_space, pl.BlockSpec(memory_space=pltpu.HBM), any_space, scalars, scalars],
        out_specs=(any_space, any_space),
        scratch_shapes=[
            pltpu.VMEM((ROWS, WIDTH), bf16),
            pltpu.VMEM((ROWS, WIDTH), bf16),
            pltpu.VMEM((8, ROWS, 2, 128), bf16),
            pltpu.VMEM((2, ROWS, HIDDEN), bf16),
            pltpu.VMEM((2, 4, 4, 64, ROWS), bf16),
            pltpu.VMEM((4, 4, 64, ROWS), bf16),
            pltpu.VMEM((8, 2, 2, 64, WIDTH), bf16),
            pltpu.VMEM((2, ROWS, 2, 128), bf16),
            pltpu.VMEM((8, 2, WIDTH), f32),
            pltpu.VMEM((4, 4, 64, SPLIT[1]), f32),
            tuple(ring_scratch(256, cols, bf16) for cols in SPLIT),
            (
                direct_scratch(64, SPLIT[0], bf16),
                direct_scratch(64, SPLIT[1], bf16),
                direct_scratch(16, WIDE, f32),
            ),
            (pltpu.VMEM((256, SPLIT[0]), f32), pltpu.VMEM((256, SPLIT[1]), f32), pltpu.VMEM((64, WIDE), f32)),
            dma((CHUNKS,)), dma((8,)), dma((2,)), dma((8,)), dma,
            dma((CHUNKS,)), dma((CHUNKS,)), dma((6,)), dma((6,)),
            dma((13,)), dma((8, 2)), dma((8, 2)), dma((8, 2)), dma((2,)), dma((2,)),
        ],
        compiler_params=pltpu.CompilerParams(
            collective_id=0, has_side_effects=True, vmem_limit_bytes=60 * 2**20
        ),
        cost_estimate=pl.CostEstimate(flops=24 * 10**9, bytes_accessed=30 * 10**6, transcendentals=0),
    )(cot, pre, w, expert, fill)


def hand_on(act_in, wgrad_in, act_out, wgrad_out, act_buf, wgrad_buf, in_sems, out_sems):
    parts = 8
    rows = ROWS // parts
    slices = [pl.ds(i * rows, rows) for i in range(parts)]
    ins = [pltpu.make_async_copy(act_in.at[r], act_buf.at[r], in_sems.at[i]) for i, r in enumerate(slices)]
    outs = [pltpu.make_async_copy(act_buf.at[r], act_out.at[r], out_sems.at[i]) for i, r in enumerate(slices)]
    ins.append(pltpu.make_async_copy(wgrad_in, wgrad_buf, in_sems.at[parts]))
    outs.append(pltpu.make_async_copy(wgrad_buf, wgrad_out, out_sems.at[parts]))
    for copy in ins:
        copy.start()
    for came, copy in zip(ins, outs):
        came.wait()
        copy.start()
    for copy in outs:
        copy.wait()


def body(cotangent, pre_act, down_weight, tile_expert, tile_fill):
    results = call(
        cotangent, pre_act, jnp.swapaxes(down_weight, 0, 1), tile_expert, tile_fill
    )
    any_space = pl.BlockSpec(memory_space=pl.ANY)
    return pl.pallas_call(
        hand_on,
        out_shape=tuple(jax.ShapeDtypeStruct(r.shape, r.dtype) for r in results),
        in_specs=[pl.BlockSpec(memory_space=pltpu.HBM)] * 2,
        out_specs=(any_space,) * 2,
        scratch_shapes=[
            pltpu.VMEM((ROWS, 2, HIDDEN), bf16), pltpu.VMEM((8, 2, WIDTH), f32),
            pltpu.SemaphoreType.DMA((9,)), pltpu.SemaphoreType.DMA((9,)),
        ],
        compiler_params=pltpu.CompilerParams(vmem_limit_bytes=60 * 2**20),
    )(*results)


def solution(mesh):
    placed = (
        P(("group", "blk"), None),
        P(("group", "blk"), None, None),
        P("blk", None, None),
        P(("group", "blk")),
        P(("group", "blk")),
    )
    return jax.shard_map(
        body,
        mesh=mesh,
        in_specs=placed,
        out_specs=(P(("group", "blk"), None, None), P(("group", "blk"), None, None)),
        check_vma=False,
    )
```

```python
import functools

import jax
import jax.numpy as jnp
from jax import lax
from jax.experimental import pallas as pl
from jax.experimental.pallas import tpu as pltpu
from jax.sharding import PartitionSpec as P

MESH = pl.DeviceIdType.MESH
grad_factor = 0.015625

ROWS = 768
HIDDEN = 1024
WIDTH = 3584
WIDE = 512
CHUNKS = WIDTH // WIDE
SPLIT = (256, 256)
f32 = jnp.float32
bf16 = jnp.bfloat16

EVENTS = {0: ((1, 0), (2, 1)), 1: ((4, 0),), 2: ((1, 1),), 3: ((2, 0),), 4: ((3, 0), (4, 1)), 5: ((5, 0),),
          6: ((3, 1), (6, 1)), 7: ((5, 1),), 8: ((6, 0),), 9: ((7, 0), (7, 1))}
HOPS = (0, 3)
ORDER = (0, 1, 2, 4, 3, 5, 6, 7)
TURNS = {2: (0, 1), 3: (2,), 5: (3,), 6: (4,), 7: (5,), 9: (6,), 10: (7,)}


def kernel(
    cot_hbm, pre_hbm, w_hbm, expert_ref, fill_ref,
    act_hbm, wgrad_hbm,
    cot_own, cot_sib, raw, pre, lhs, lhs_sib, w_all, grad_buf, out_buf, mixed,
    rings, directs, tot,
    cot_sem, pre_sem, w_sem, grad_sem, out_sem,
    cs_send, cs_recv, ls_send, ls_recv,
    ag_send, ag_recv, sib_send, sib_recv, hop_send, hop_recv,
):
    g = lax.axis_index("group")
    b = lax.axis_index("blk")
    x_lo, z = lax.div(g, 4), lax.rem(g, 4)
    y, c = lax.div(b, 4), lax.rem(b, 2)
    x_hi = lax.rem(lax.div(b, 2), 2)
    x = x_hi * 2 + x_lo

    def device(dx, dy, dz, core):
        xx, yy, zz = lax.rem(x + dx, 4), lax.rem(y + dy, 4), lax.rem(z + dz, 4)
        return (lax.rem(xx, 2) * 4 + zz, yy * 4 + lax.div(xx, 2) * 2 + core)

    other = 1 - c
    sibling = device(0, 0, 0, other)
    x_up, x_dn = device(1, 0, 0, c), device(3, 0, 0, c)
    y_up, y_dn = device(0, 1, 0, c), device(0, 3, 0, c)
    z_up, z_dn = device(0, 0, 1, c), device(0, 0, 3, c)
    x_far, y_far, z_far = device(2, 0, 0, c), device(0, 2, 0, c), device(0, 0, 2, c)
    x_peer = device(3 - 2 * x + 4, 0, 0, c)

    barrier = pltpu.get_barrier_semaphore()
    for peer in (sibling, x_up, x_dn, x_far, y_up, y_dn, y_far, z_up, z_dn, z_far):
        pl.semaphore_signal(barrier, inc=1, device_id=peer, device_id_type=MESH)

    def cot_cols(k):
        return pl.ds(pl.multiple_of(k * WIDE, WIDE), WIDE)

    def cot_copy(k):
        return pltpu.make_async_copy(cot_hbm.at[:, cot_cols(k)], cot_own.at[:, cot_cols(k)], cot_sem.at[k])

    def pre_copy(part):
        cols = pl.ds(pl.multiple_of(part * 128, 128), 128)
        return pltpu.make_async_copy(pre_hbm.at[:, :, cols], raw.at[part], pre_sem.at[part])

    q_own = y * 2 + x_hi

    def w_copy(e):
        return pltpu.make_async_copy(w_hbm.at[e], w_all.at[q_own, e, c], w_sem.at[e])

    for e in range(2):
        w_copy(e).start()

    @pl.loop(0, 8)
    def _(part):
        pre_copy(part).start()

    @pl.loop(0, CHUNKS)
    def _(k):
        cot_copy(k).start()

    pl.semaphore_wait(barrier, 10)

    def remote(src, dst, send, recv, device_id):
        return pltpu.make_async_remote_copy(
            src_ref=src, dst_ref=dst, send_sem=send, recv_sem=recv, device_id=device_id, device_id_type=MESH
        )

    def lhs_remote(t):
        rows = pl.ds(pl.multiple_of(t * 128, 128), 128)
        return remote(
            lhs.at[1, :, :, :, rows], lhs_sib.at[:, :, :, rows], ls_send.at[t], ls_recv.at[t], sibling
        )

    def cot_remote(k):
        return remote(
            cot_hbm.at[:, cot_cols(k)], cot_sib.at[:, cot_cols(k)], cs_send.at[k], cs_recv.at[k], sibling
        )

    def piece(j):
        yy = lax.rem(y + (0, 3, 1, 2)[j % 4], 4)
        return yy * 2 + (x_hi if j < 4 else 1 - x_hi)

    def gather(slot):
        src_j, dst_j, e, device_id = sends[slot]
        block = w_all.at[piece(src_j), e, c]
        return remote(block, block, ag_send.at[slot], ag_recv.at[dst_j, e], device_id)

    def hop(i):
        block = w_all.at[piece(0), 1, c, pl.ds(i * 32, 32)]
        return remote(block, block, hop_send.at[i], hop_recv.at[i], x_peer)

    def hop_wait(i):
        block = w_all.at[piece(4), 1, c, pl.ds(i * 32, 32)]
        remote(block, block, hop_send.at[i], hop_recv.at[i], x_peer).wait_recv()

    def gather_wait(j, e):
        if (j, e) == (4, 1):
            for i in range(2):
                hop_wait(i)
        else:
            block = w_all.at[piece(j), e, c]
            remote(block, block, ag_send.at[0], ag_recv.at[j, e], sibling).wait_recv()

    def share(j, e):
        block = w_all.at[piece(j), e, c]
        return remote(block, block, sib_send.at[j, e], sib_recv.at[j, e], sibling)

    def share_wait(j, e):
        block = w_all.at[piece(j), e, other]
        remote(block, block, sib_send.at[j, e], sib_recv.at[j, e], sibling).wait_recv()

    sends = [(0, 1, 0, y_up), (0, 2, 1, y_dn), (0, 4, 0, x_peer), (0, 1, 1, y_up), (0, 2, 0, y_dn)]
    sends += [(1, 3, 0, y_up), (2, 3, 1, y_dn)]
    for e in range(2):
        sends += [(4, 5, e, y_up), (4, 6, e, y_dn)]
    sends += [(5, 7, 0, y_up), (6, 7, 1, y_dn)]

    def gather_start(j, e):
        for slot, (src_j, _, src_e, _) in enumerate(sends):
            if (src_j, src_e) == (j, e):
                gather(slot).start()

    def arrived(j, e):
        gather_wait(j, e)
        gather_start(j, e)
        share(j, e).start()

    cot_remote(0).start()
    for e in range(2):
        w_copy(e).wait()
    for slot in range(5):
        gather(slot).start()

    for part in range(8):
        pre_copy(part).wait()

        @pl.loop(0, ROWS // 128)
        def _(t):
            rows = pl.ds(pl.multiple_of(t * 128, 128), 128)
            both = raw[part, rows].astype(f32)
            for i in range(2):
                pre[i, rows, part * 128:part * 128 + 128] = both[:, i, :].astype(bf16)

    @pl.loop(0, ROWS // 128)
    def _(t):
        rows = pl.ds(pl.multiple_of(t * 128, 128), 128)
        lane = lax.broadcasted_iota(jnp.int32, (8, 128), 1)
        alive = lane < fill_ref[t]
        chosen = jnp.zeros((8, 128), jnp.int32) + expert_ref[t]
        masks = [jnp.logical_and(alive, chosen == e) for e in range(2)]

        @pl.loop(0, 8)
        def _(part):
            cols = pl.ds(pl.multiple_of(part * 128, 128), 128)
            gate = pre[0, rows, cols].astype(f32)
            up = pre[1, rows, cols].astype(f32)
            sig = jax.nn.sigmoid(gate)
            turned = jnp.transpose(gate * sig * up)
            part_x, part_z = lax.div(part, 4), lax.rem(part, 4)
            for yy in range(4):
                for hi in range(2):
                    for core in range(2):
                        at = yy * 32 + hi * 16 + core * 8
                        value = turned[at:at + 8]
                        pair = jnp.concatenate([jnp.where(mask, value, 0.0) for mask in masks], axis=0)
                        lhs[lax.rem(c + core, 2), part_z, hi * 2 + part_x, yy * 16:yy * 16 + 16, rows] = pair.astype(bf16)

        lhs_remote(t).start()

    @pl.loop(1, CHUNKS)
    def _(k):
        cot_remote(k).start()

    for e in range(2):
        share(0, e).start()

    z_ring, x_ring, y_ring = (z, z_up, z_dn, z_far), (x, x_up, x_dn, x_far), (y, y_up, y_dn, y_far)
    ring_of = (z_ring, x_ring)
    direct_of = (x_ring, z_ring, y_ring)

    def far_copy(st, k, half):
        far, rfar, send, recv = (rings[st][i] for i in (0, 3, 8, 9))
        rows = far.shape[1] // 2
        return remote(
            far.at[k, pl.ds(half * rows, rows)], rfar.at[k, pl.ds(half * rows, rows)],
            send.at[k, half], recv.at[k, half], ring_of[st][1 + half],
        )

    def near_copy(st, k, way):
        src, dst, send, recv = (rings[st][i] for i in (1 + way, 4 + way, 8, 9))
        return remote(src.at[k], dst.at[k], send.at[k, 2 + way], recv.at[k, 2 + way], ring_of[st][1 + way])

    def emit(st, k, offset, value):
        far, up, dn, _, _, _, own, rel, _, _ = rings[st]
        half = far.shape[1] // 2
        kind = far.dtype
        if offset == 2:
            far[k] = value.astype(kind)
            far_copy(st, k, 0).start()
            far_copy(st, k, 1).start()
        elif offset == 1:
            rel[lax.rem(k, 2), 0] = value[:half]
            up[k, half:] = value[half:].astype(kind)
        elif offset == 3:
            rel[lax.rem(k, 2), 1] = value[half:]
            dn[k, :half] = value[:half].astype(kind)
        else:
            own[lax.rem(k, 4)] = value

    def relay(k):
        for st in range(2):
            _, up, dn, rfar, _, _, _, rel, _, _ = rings[st]
            half = up.shape[1] // 2
            kind = up.dtype
            far_copy(st, k, 0).wait_recv()
            up[k, :half] = (rel[lax.rem(k, 2), 0] + rfar[k, :half].astype(f32)).astype(kind)
            near_copy(st, k, 0).start()
            far_copy(st, k, 1).wait_recv()
            dn[k, half:] = (rel[lax.rem(k, 2), 1] + rfar[k, half:].astype(f32)).astype(kind)
            near_copy(st, k, 1).start()

    def total(st, k):
        near_copy(st, k, 0).wait_recv()
        near_copy(st, k, 1).wait_recv()
        _, _, _, _, rup, rdn, own, _, _, _ = rings[st]
        return own[lax.rem(k, 4)] + rup[k].astype(f32) + rdn[k].astype(f32)

    def direct_copy(st, k, i):
        out, came, _, send, recv = directs[st]
        return remote(out.at[k, i], came.at[k, i], send.at[k, i], recv.at[k, i], direct_of[st][1 + i])

    def spread(st, k, load):
        out, _, own, _, _ = directs[st]
        for i, offset in ((2, 2), (0, 1), (1, 3)):
            out[k, i] = load(lax.rem(direct_of[st][0] + offset, 4)).astype(out.dtype)
            direct_copy(st, k, i).start()
        own[k] = load(direct_of[st][0])

    def collected(st, k):
        _, came, own, _, _ = directs[st]
        for i in range(3):
            direct_copy(st, k, i).wait_recv()
        return own[k] + came[k, 0].astype(f32) + came[k, 1].astype(f32) + came[k, 2].astype(f32)

    def make(k):
        cot_remote(k).wait_recv()
        cols = cot_cols(k)
        for offset in (2, 1, 3, 0):
            at = lax.rem(z + offset, 4)
            value = jnp.dot(lhs[0, at].reshape(256, ROWS), cot_own[:, cols], preferred_element_type=f32)
            value += jnp.dot(lhs_sib[at].reshape(256, ROWS), cot_sib[:, cols], preferred_element_type=f32)
            emit(0, k, offset, value[:, :SPLIT[0]])
            mixed[at] = value[:, SPLIT[0]:].reshape(4, 64, SPLIT[1])
        for offset in (2, 1, 3, 0):
            at = lax.rem(x + offset, 4)
            emit(1, k, offset, mixed[:, at].reshape(256, SPLIT[1]))

    def onward(k):
        for st in range(2):
            tot[st][...] = total(st, k)
            spread(st, k, lambda at: tot[st][pl.ds(pl.multiple_of(at * 64, 64), 64), :])

    def joined(k):
        for st in range(2):
            tot[2][:, st * SPLIT[0]:st * SPLIT[0] + SPLIT[st]] = collected(st, k)
        spread(2, k, lambda at: tot[2][pl.ds(pl.multiple_of(at * 16, 16), 16), :])

    def last(k):
        value = collected(2, k) * grad_factor
        for e in range(2):
            out_buf[:, e, cot_cols(k)] = value[e * 8:e * 8 + 8]

    def grad_copy(turn):
        cols = pl.ds(pl.multiple_of(piece(ORDER[turn]) * 128, 128), 128)
        return pltpu.make_async_copy(grad_buf.at[turn % 2], act_hbm.at[:, :, cols], grad_sem.at[turn])

    def hidden(turn):
        j = ORDER[turn]
        for e in range(2):
            share_wait(j, e)
        if turn >= 2:
            grad_copy(turn - 2).wait()
        q = piece(j)
        cols = pl.ds(pl.multiple_of(q * 128, 128), 128)

        @pl.loop(0, ROWS // 256)
        def _(m):
            rows = pl.ds(pl.multiple_of(m * 256, 256), 256)
            each = lax.dot_general(
                cot_own[rows, :], w_all[q].reshape(256, WIDTH), (((1,), (1,)), ((), ())), preferred_element_type=f32
            )
            for i in range(2):
                part = pl.ds(pl.multiple_of(m * 256 + i * 128, 128), 128)
                row = lax.broadcasted_iota(jnp.int32, (128, 128), 0)
                alive = row < fill_ref[m * 2 + i]
                second = jnp.zeros((128, 128), jnp.int32) + expert_ref[m * 2 + i] == 1
                both = each[i * 128:(i + 1) * 128]
                grad = jnp.where(alive, jnp.where(second, both[:, 128:], both[:, :128]), 0.0)
                gate = pre[0, part, cols].astype(f32)
                up = pre[1, part, cols].astype(f32)
                sig = jax.nn.sigmoid(gate)
                grad_buf[turn % 2, part, 0, :] = (grad * up * sig * (1.0 + gate * (1.0 - sig))).astype(bf16)
                grad_buf[turn % 2, part, 1, :] = (grad * (gate * sig)).astype(bf16)

        grad_copy(turn).start()

    @pl.loop(0, CHUNKS)
    def _(k):
        cot_copy(k).wait()

    @pl.loop(0, ROWS // 128)
    def _(t):
        lhs_remote(t).wait_recv()

    @pl.loop(0, CHUNKS + 4)
    def _(t):
        def at(lag, do):
            @pl.when(jnp.logical_and(t >= lag, t < CHUNKS + lag))
            def _():
                do(t - lag)

        def on(when, do):
            @pl.when(t == when)
            def _():
                do()

        for i in range(2):
            on(HOPS[i], lambda: hop(i).start())
        for when, those in EVENTS.items():
            for j, e in those:
                on(when, functools.partial(arrived, j, e))
        at(0, make)
        at(1, relay)
        at(2, onward)
        at(4, joined)

        for when, those in TURNS.items():
            for turn in those:
                on(when, functools.partial(hidden, turn))

    @pl.loop(0, CHUNKS)
    def _(k):
        last(k)

    out = pltpu.make_async_copy(out_buf, wgrad_hbm, out_sem)
    out.start()
    for turn in (6, 7):
        grad_copy(turn).wait()
    out.wait()

    @pl.loop(0, ROWS // 128)
    def _(t):
        lhs_remote(t).wait_send()

    @pl.loop(0, CHUNKS)
    def _(k):
        cot_remote(k).wait_send()
        for st in range(2):
            for i in range(2):
                far_copy(st, k, i).wait_send()
                near_copy(st, k, i).wait_send()
        for st in range(3):
            for i in range(3):
                direct_copy(st, k, i).wait_send()

    for slot in range(len(sends)):
        gather(slot).wait_send()
    for i in range(2):
        hop(i).wait_send()
    for j in range(8):
        for e in range(2):
            share(j, e).wait_send()


def ring_scratch(rows, cols, kind):
    dma = pltpu.SemaphoreType.DMA
    return (
        *[pltpu.VMEM((CHUNKS, rows, cols), kind)] * 6,
        pltpu.VMEM((4, rows, cols), f32),
        pltpu.VMEM((2, 2, rows // 2, cols), f32),
        dma((CHUNKS, 4)),
        dma((CHUNKS, 4)),
    )


def direct_scratch(rows, cols, kind):
    dma = pltpu.SemaphoreType.DMA
    return (
        pltpu.VMEM((CHUNKS, 3, rows, cols), kind),
        pltpu.VMEM((CHUNKS, 3, rows, cols), kind),
        pltpu.VMEM((CHUNKS, rows, cols), f32),
        dma((CHUNKS, 3)),
        dma((CHUNKS, 3)),
    )


def call(cot, pre, w, expert, fill):
    dma = pltpu.SemaphoreType.DMA
    any_space = pl.BlockSpec(memory_space=pl.ANY)
    scalars = pl.BlockSpec(memory_space=pltpu.SMEM)
    return pl.pallas_call(
        kernel,
        out_shape=(
            jax.ShapeDtypeStruct((ROWS, 2, HIDDEN), bf16),
            jax.ShapeDtypeStruct((8, 2, WIDTH), f32),
        ),
        in_specs=[any_space, pl.BlockSpec(memory_space=pltpu.HBM), any_space, scalars, scalars],
        out_specs=(any_space, any_space),
        scratch_shapes=[
            pltpu.VMEM((ROWS, WIDTH), bf16),
            pltpu.VMEM((ROWS, WIDTH), bf16),
            pltpu.VMEM((8, ROWS, 2, 128), bf16),
            pltpu.VMEM((2, ROWS, HIDDEN), bf16),
            pltpu.VMEM((2, 4, 4, 64, ROWS), bf16),
            pltpu.VMEM((4, 4, 64, ROWS), bf16),
            pltpu.VMEM((8, 2, 2, 64, WIDTH), bf16),
            pltpu.VMEM((2, ROWS, 2, 128), bf16),
            pltpu.VMEM((8, 2, WIDTH), f32),
            pltpu.VMEM((4, 4, 64, SPLIT[1]), f32),
            tuple(ring_scratch(256, cols, bf16) for cols in SPLIT),
            (
                direct_scratch(64, SPLIT[0], bf16),
                direct_scratch(64, SPLIT[1], bf16),
                direct_scratch(16, WIDE, f32),
            ),
            (pltpu.VMEM((256, SPLIT[0]), f32), pltpu.VMEM((256, SPLIT[1]), f32), pltpu.VMEM((64, WIDE), f32)),
            dma((CHUNKS,)), dma((8,)), dma((2,)), dma((8,)), dma,
            dma((CHUNKS,)), dma((CHUNKS,)), dma((6,)), dma((6,)),
            dma((13,)), dma((8, 2)), dma((8, 2)), dma((8, 2)), dma((2,)), dma((2,)),
        ],
        compiler_params=pltpu.CompilerParams(
            collective_id=0, has_side_effects=True, vmem_limit_bytes=60 * 2**20
        ),
        cost_estimate=pl.CostEstimate(flops=24 * 10**9, bytes_accessed=30 * 10**6, transcendentals=0),
    )(cot, pre, w, expert, fill)


def hand_on(act_in, wgrad_in, act_out, wgrad_out, act_buf, wgrad_buf, in_sems, out_sems):
    parts = 8
    rows = ROWS // parts
    slices = [pl.ds(i * rows, rows) for i in range(parts)]
    ins = [pltpu.make_async_copy(act_in.at[r], act_buf.at[r], in_sems.at[i]) for i, r in enumerate(slices)]
    outs = [pltpu.make_async_copy(act_buf.at[r], act_out.at[r], out_sems.at[i]) for i, r in enumerate(slices)]
    ins.append(pltpu.make_async_copy(wgrad_in, wgrad_buf, in_sems.at[parts]))
    outs.append(pltpu.make_async_copy(wgrad_buf, wgrad_out, out_sems.at[parts]))
    for copy in ins:
        copy.start()
    for came, copy in zip(ins, outs):
        came.wait()
        copy.start()
    for copy in outs:
        copy.wait()


def body(cotangent, pre_act, down_weight, tile_expert, tile_fill):
    results = call(
        cotangent, pre_act, jnp.swapaxes(down_weight, 0, 1), tile_expert, tile_fill
    )
    any_space = pl.BlockSpec(memory_space=pl.ANY)
    return pl.pallas_call(
        hand_on,
        out_shape=tuple(jax.ShapeDtypeStruct(r.shape, r.dtype) for r in results),
        in_specs=[pl.BlockSpec(memory_space=pltpu.HBM)] * 2,
        out_specs=(any_space,) * 2,
        scratch_shapes=[
            pltpu.VMEM((ROWS, 2, HIDDEN), bf16), pltpu.VMEM((8, 2, WIDTH), f32),
            pltpu.SemaphoreType.DMA((9,)), pltpu.SemaphoreType.DMA((9,)),
        ],
        compiler_params=pltpu.CompilerParams(vmem_limit_bytes=60 * 2**20),
    )(*results)


def solution(mesh):
    placed = (
        P(("group", "blk"), None),
        P(("group", "blk"), None, None),
        P("blk", None, None),
        P(("group", "blk")),
        P(("group", "blk")),
    )
    return jax.shard_map(
        body,
        mesh=mesh,
        in_specs=placed,
        out_specs=(P(("group", "blk"), None, None), P(("group", "blk"), None, None)),
        check_vma=False,
    )
```
